32 devices in a mesh: sub: 16 (over z, y, x), node: 2 (over core).
Axes of the slice: x: 2, y: 2, z: 4, core: 2. Of those that a mesh axis runs over, the one named last changes fastest.
Arguments:
- search_vectors: float32 [16384, 256], P('sub'), may hold values from -60 to 60
- ritz_values: float32 [256], replicated, may hold values from -0.9 to 0.9
- matrix_blocks: float32 [128, 4, 128, 128], P('sub'), may hold values from -0.25 to 0.25
- block_lists: int32 [128, 4], P('sub'), may hold values from 0 to 127, as said below
- inverses: float32 [4, 2, 128, 128, 128], P('node', None, 'sub'), may hold values from -0.5 to 0.5
- panels: float32 [16, 512, 1024], P('sub'), may hold values from -0.1875 to 0.1875
- separator_map: int32 [16, 4], P('sub'), may hold values from 0 to 7, as said below
- separator_shift: float32 [1024], replicated, may hold values from -0.9 to 0.9
Outputs:
- normalized_vectors: float32 [16384, 256], P('sub', 'node')
The draws below stay inside these ranges and needn't reach their ends.
Inputs may be any that keep to these rules, and one draw needn't show every extreme that they name: `block_lists`: entry 0 of row g is g; the other entries of row g are distinct blocks from g - 4 to g + 4, none equal to g. `separator_map`: the entries of one row are distinct.
All inputs are finite; a program needn't handle non-finite values.
Results may differ from the reference program's by a relative error of at most 0.0001.
Values sent between devices are 32-bit elements; how exact they have to be, the bound alone decides.
A program may use at most 64 MiB of HBM per device.

```python
import math
import jax
import jax.numpy as jnp
from jax import lax

VECS = 256
BLK = 128
ROWS = 1024
DEGREE = 4
HALO_BLOCKS = 4
SEP = 512
SEP_GROUPS = 8
NODES = 4
SUBS = 16
NROWS = 16384
NBLK = 8
BLOCKS = 128
SEP_BLOCKS = 4
GSEP = 1024


def draw_search_vectors(key, part):
    positions = jnp.arange(NROWS, dtype=jnp.float32) / max(NROWS - 1, 1)
    row_scale = jnp.exp(jnp.log(3.0) * positions)[:, None]
    values = jax.random.normal(jax.random.fold_in(key, 24), (NROWS, VECS), jnp.float32) * row_scale
    return jnp.clip(values, -60.0, 60.0)


def draw_block_lists(key, part):
    random_bits = jax.random.randint(jax.random.fold_in(key, 31), (BLOCKS, 2 * HALO_BLOCKS), 0, 2 ** 20, dtype=jnp.int32)
    offsets = jnp.concatenate([jnp.arange(-HALO_BLOCKS, 0, dtype=jnp.int32), jnp.arange(1, HALO_BLOCKS + 1, dtype=jnp.int32)])
    own_block = jnp.arange(BLOCKS, dtype=jnp.int32)[:, None]
    targets = own_block + offsets[None, :]
    valid = ((targets >= 0) & (targets < BLOCKS)).astype(jnp.int32)
    scores = random_bits * (2 * HALO_BLOCKS) + jnp.arange(2 * HALO_BLOCKS, dtype=jnp.int32)[None, :] + valid * 2 ** 26
    chosen_idx = lax.top_k(scores, DEGREE - 1)[1]
    chosen = jnp.take_along_axis(targets, chosen_idx, axis=1)
    return jnp.concatenate([own_block, chosen], axis=1).astype(jnp.int32)


def draw_separator_map(key, part):
    random_bits = jax.random.randint(jax.random.fold_in(key, 41), (SUBS, SEP_GROUPS), 0, 2 ** 20, dtype=jnp.int32)
    scores = random_bits * SEP_GROUPS + jnp.arange(SEP_GROUPS, dtype=jnp.int32)[None, :]
    return lax.top_k(scores, SEP_BLOCKS)[1].astype(jnp.int32)


def levels(stream_key, shape, pieces, least, largest):
    loudness = 1.0
    for position, shards_of in pieces:
        steps = jax.random.uniform(jax.random.fold_in(jax.random.fold_in(stream_key, 6), position), (shards_of,), jnp.float32, least / len(pieces), largest / len(pieces))
        loudness = loudness * jnp.repeat(jnp.exp(steps), shape[position] // shards_of).reshape((-1,) + (1,) * (len(shape) - 1 - position))
    return loudness


def noise(rng, dims, width, reach, cuts=(), kind=jnp.bfloat16):
    array = jax.random.normal(rng, dims, jnp.float32) * width
    if len(cuts) > 0:
        array = levels(rng, dims, cuts, -0.22, 0.18) * array
    return jnp.clip(array, min=-reach, max=reach).astype(kind)


def setup_inputs(seed: int = 0) -> dict:
    splits = jax.random.split(jax.random.key(seed), 9)
    search_vectors = draw_search_vectors(jax.random.fold_in(splits[8], 71), 0)
    ritz_values = jnp.clip(jax.random.uniform(splits[1], (VECS,), jnp.float32, -0.9, 0.9), -0.9, 0.9)
    matrix_blocks = noise(splits[2], (BLOCKS, DEGREE, BLK, BLK), (DEGREE * BLK) ** -0.5, 0.25, ((0, 16),), jnp.float32)
    block_lists = draw_block_lists(jax.random.fold_in(splits[8], 71), 0)
    inverses = noise(splits[4], (NODES, 2, BLOCKS, BLK, BLK), BLK ** -0.5, 0.5, ((0, 2), (2, 16)), jnp.float32)
    panels = noise(splits[5], (SUBS, SEP, ROWS), ROWS ** -0.5, 0.1875, ((0, 16),), jnp.float32)
    separator_map = draw_separator_map(jax.random.fold_in(splits[8], 71), 0)
    separator_shift = jnp.clip(jax.random.uniform(splits[7], (GSEP,), jnp.float32, -0.9, 0.9), -0.9, 0.9)
    return dict(search_vectors=search_vectors, ritz_values=ritz_values, matrix_blocks=matrix_blocks, block_lists=block_lists, inverses=inverses, panels=panels, separator_map=separator_map, separator_shift=separator_shift)


HIGHEST = lax.Precision.HIGHEST

def reference(search_vectors, ritz_values, matrix_blocks, block_lists, inverses, panels, separator_map, separator_shift):
    by_block = search_vectors.reshape(BLOCKS, BLK, VECS)

    def local_rows(operands):
        matrices, listed = operands
        return jnp.einsum('bkij,bkjm->bim', matrices, by_block[listed], precision=HIGHEST)
    product = lax.map(local_rows, (matrix_blocks.reshape(SUBS, NBLK, DEGREE, BLK, BLK), block_lists.reshape(SUBS, NBLK, DEGREE)))
    residual = product.reshape(NROWS, VECS) - search_vectors * ritz_values[None, :]
    res_blocks = residual.reshape(BLOCKS, BLK, VECS)
    one_hot = (separator_map[:, :, None] == jnp.arange(SEP_GROUPS, dtype=jnp.int32)[None, None, :]).astype(jnp.float32)
    weighted = jnp.zeros((NROWS, VECS), jnp.float32)
    for node_number in range(NODES):
        angle = math.pi * (node_number + 0.5) / NODES
        real_shift = math.cos(angle)
        imag_shift = math.sin(angle)
        first_guess = jnp.einsum('cbij,bjm->cbim', inverses[node_number], res_blocks, precision=HIGHEST)
        first_guess = first_guess.reshape(2, SUBS, ROWS, VECS)
        partial_value = jnp.einsum('tsr,ctrm->ctsm', panels, first_guess, precision=HIGHEST).reshape(2, SUBS, SEP_BLOCKS, BLK, VECS)
        separator = jnp.einsum('tpg,ctpkm->cgkm', one_hot, partial_value, precision=HIGHEST).reshape(2, GSEP, VECS)
        real_gap = (real_shift - separator_shift)[:, None]
        modulus = real_gap * real_gap + imag_shift * imag_shift
        real_part = separator[0]
        imag_part = separator[1]
        coarse = jnp.stack([(real_part * real_gap + imag_part * imag_shift) / modulus, (imag_part * real_gap - real_part * imag_shift) / modulus]).reshape(2, SEP_GROUPS, BLK, VECS)
        picked = jnp.einsum('tpg,cgkm->ctpkm', one_hot, coarse, precision=HIGHEST).reshape(2, SUBS, SEP, VECS)
        correction = jnp.einsum('tsr,ctsm->ctrm', panels, picked, precision=HIGHEST).reshape(2, BLOCKS, BLK, VECS)
        products = jnp.einsum('cbij,dbjm->cdbim', inverses[node_number], correction, precision=HIGHEST).reshape(2, 2, NROWS, VECS)
        first_flat = first_guess.reshape(2, NROWS, VECS)
        sol_real = first_flat[0] - (products[0, 0] - products[1, 1])
        sol_imag = first_flat[1] - (products[0, 1] + products[1, 0])
        weight_real = 2.0 * real_shift / NODES
        weight_imag = 2.0 * imag_shift / NODES
        weighted = weighted + weight_real * sol_real - weight_imag * sol_imag
    update = search_vectors - weighted
    factor = lax.rsqrt(lax.optimization_barrier(jnp.mean(update * update, axis=0)) + 1e-06)
    return update * factor[None, :]
```

```python
import functools
import math

import jax
import jax.numpy as jnp
from jax import lax
from jax.experimental import pallas as pl
from jax.experimental.pallas import tpu as pltpu
from jax.sharding import PartitionSpec as P

HALO_BLOCKS = 4
SEP_GROUPS = 8
HIGH = lax.Precision.HIGH
VMEM = pltpu.VMEM
SMEM = pltpu.SMEM


def split(x):
    hi = x.astype(jnp.bfloat16)
    lo = (x - hi.astype(jnp.float32)).astype(jnp.bfloat16)
    return hi, lo


def dot3(a, b):
    a_hi, a_lo = split(a)
    b_hi, b_lo = split(b)
    dot = functools.partial(jnp.dot, preferred_element_type=jnp.float32)
    return dot(a_hi, b_hi) + (dot(a_hi, b_lo) + dot(a_lo, b_hi))


def meet(targets):
    barrier = pltpu.get_barrier_semaphore()
    for target in targets:
        pl.semaphore_signal(
            barrier, inc=1, device_id=target, device_id_type=pl.DeviceIdType.MESH
        )
    pl.semaphore_wait(barrier, len(targets))


def remote(src, dst, send, recv, target):
    return pltpu.make_async_remote_copy(
        src_ref=src,
        dst_ref=dst,
        send_sem=send,
        recv_sem=recv,
        device_id=target,
        device_id_type=pl.DeviceIdType.MESH,
    )


def residual_kernel(
    subs, nodes, index_ref, own_ref, ritz_ref, blocks_ref, out_ref,
    padded, halo_send, halo_recv, own_sem, node_send, node_recv,
):
    sub, node = lax.axis_index("sub"), lax.axis_index("node")
    count = own_ref.shape[0]
    after, before = lax.rem(sub + 1, subs), lax.rem(sub + subs - 1, subs)
    others = [lax.rem(node + k, nodes) for k in range(1, nodes)]
    meet([{"sub": after}, {"sub": before}] + [{"node": o} for o in others])
    up = remote(
        own_ref.at[pl.ds(count - HALO_BLOCKS, HALO_BLOCKS)],
        padded.at[pl.ds(0, HALO_BLOCKS)],
        halo_send.at[0], halo_recv.at[0], {"sub": after},
    )
    down = remote(
        own_ref.at[pl.ds(0, HALO_BLOCKS)],
        padded.at[pl.ds(HALO_BLOCKS + count, HALO_BLOCKS)],
        halo_send.at[1], halo_recv.at[1], {"sub": before},
    )
    up.start()
    down.start()
    mine = pltpu.make_async_copy(own_ref, padded.at[pl.ds(HALO_BLOCKS, count)], own_sem)
    mine.start()
    mine.wait()
    up.wait()
    down.wait()

    def copies(b):
        return [
            remote(
                out_ref.at[node, b], out_ref.at[node, b],
                node_send.at[k, b], node_recv.at[k, b], {"node": o},
            )
            for k, o in enumerate(others)
        ]

    def step(b, carry):
        total = -(own_ref[b] * ritz_ref[...])
        for q in range(blocks_ref.shape[1]):
            total = total + dot3(blocks_ref[b, q], padded[index_ref[b, q]])
        out_ref[node, b] = total
        for copy in copies(b):
            copy.start()
        return carry

    lax.fori_loop(0, count, step, 0)

    def finish(b, carry):
        for copy in copies(b):
            copy.wait()
        return carry

    lax.fori_loop(0, count, finish, 0)


def residual_call(index, own, ritz, blocks, subs, nodes):
    count, size, width = own.shape
    return pl.pallas_call(
        functools.partial(residual_kernel, subs, nodes),
        out_shape=jax.ShapeDtypeStruct((nodes, count, size, width), jnp.float32),
        in_specs=[pl.BlockSpec(memory_space=SMEM)] + [pl.BlockSpec(memory_space=VMEM)] * 3,
        out_specs=pl.BlockSpec(memory_space=VMEM),
        scratch_shapes=[
            VMEM((count + 2 * HALO_BLOCKS, size, width), jnp.float32),
            pltpu.SemaphoreType.DMA((2,)),
            pltpu.SemaphoreType.DMA((2,)),
            pltpu.SemaphoreType.DMA,
            pltpu.SemaphoreType.DMA((nodes - 1, count)),
            pltpu.SemaphoreType.DMA((nodes - 1, count)),
        ],
        compiler_params=pltpu.CompilerParams(collective_id=0, has_side_effects=True),
        name="residual",
    )(index, own, ritz, blocks)


def separator_kernel(
    subs, cuts, map_ref, slot_ref, shift_ref, real_ref, imag_ref, part_ref, back_ref,
    landed, coarse, picked, send, recv, own_sem,
):
    sub = lax.axis_index("sub")
    node_local, _, panels, size, width = part_ref.shape
    rows, cols = size * cuts // subs, width // cuts
    others = [lax.rem(sub + k, subs) for k in range(1, subs)]
    meet([{"sub": o} for o in others])

    def piece(ref, owner):
        row = pl.multiple_of((owner // cuts) * rows, rows)
        col = pl.multiple_of(lax.rem(owner, cuts) * cols, cols) if cuts > 1 else 0
        return ref.at[:, :, :, pl.ds(row, rows), pl.ds(col, cols)]

    there = [
        remote(
            piece(part_ref, o), landed.at[sub, :, :, pl.ds(0, panels)],
            send.at[0, k], recv.at[0, k], {"sub": o},
        )
        for k, o in enumerate(others)
    ]
    for copy in there:
        copy.start()
    own = pltpu.make_async_copy(
        piece(part_ref, sub), landed.at[sub, :, :, pl.ds(0, panels)], own_sem.at[0]
    )
    own.start()
    landed[:, :, :, panels] = jnp.zeros((subs, node_local, 2, rows, cols), jnp.float32)
    own.wait()
    for copy in there:
        copy.wait()

    def group(g, carry):
        shift = shift_ref[g]
        for n in range(node_local):
            gap = real_ref[n] - shift
            imag = imag_ref[n]
            modulus = gap * gap + imag * imag
            by_real, by_imag = gap / modulus, imag / modulus

            def add(t, sums):
                slot = slot_ref[t, g]
                return (sums[0] + landed[t, n, 0, slot], sums[1] + landed[t, n, 1, slot])

            zero = jnp.zeros((rows, cols), jnp.float32)
            real, imaginary = lax.fori_loop(0, subs, add, (zero, zero))
            coarse[g, n, 0] = real * by_real + imaginary * by_imag
            coarse[g, n, 1] = imaginary * by_real - real * by_imag
        return carry

    lax.fori_loop(0, shift_ref.shape[0], group, 0)

    def pick(t, carry):
        for p in range(panels):
            value = coarse[map_ref[t, p]]
            for n in range(node_local):
                for c in range(2):
                    picked[t, n, c, p] = value[n, c]
        return carry

    lax.fori_loop(0, subs, pick, 0)
    home = [
        remote(
            picked.at[o], piece(back_ref, sub), send.at[1, k], recv.at[1, k], {"sub": o}
        )
        for k, o in enumerate(others)
    ]
    for copy in home:
        copy.start()
    own = pltpu.make_async_copy(picked.at[sub], piece(back_ref, sub), own_sem.at[1])
    own.start()
    own.wait()
    for copy in home:
        copy.wait()


def separator_call(maps, slots, shift, real_shift, imag_shift, part, subs):
    node_local, _, panels, size, width = part.shape
    cuts = max(1, subs * 8 // size)
    rows, cols = size * cuts // subs, width // cuts
    groups = shift.shape[0] // size
    row = (lax.axis_index("sub") // cuts) * rows
    my_shift = lax.dynamic_slice_in_dim(shift.reshape(groups, size, 1), row, rows, 1)
    my_shift = jnp.broadcast_to(my_shift, (groups, rows, cols))
    return pl.pallas_call(
        functools.partial(separator_kernel, subs, cuts),
        out_shape=jax.ShapeDtypeStruct(part.shape, jnp.float32),
        in_specs=[
            pl.BlockSpec(memory_space=SMEM),
            pl.BlockSpec(memory_space=SMEM),
            pl.BlockSpec(memory_space=VMEM),
            pl.BlockSpec(memory_space=SMEM),
            pl.BlockSpec(memory_space=SMEM),
            pl.BlockSpec(memory_space=VMEM),
        ],
        out_specs=pl.BlockSpec(memory_space=VMEM),
        scratch_shapes=[
            VMEM((subs, node_local, 2, panels + 1, rows, cols), jnp.float32),
            VMEM((groups, node_local, 2, rows, cols), jnp.float32),
            VMEM((subs, node_local, 2, panels, rows, cols), jnp.float32),
            pltpu.SemaphoreType.DMA((2, subs - 1)),
            pltpu.SemaphoreType.DMA((2, subs - 1)),
            pltpu.SemaphoreType.DMA((2,)),
        ],
        compiler_params=pltpu.CompilerParams(collective_id=1, has_side_effects=True),
        name="separator",
    )(maps, slots, my_shift, real_shift, imag_shift, part)


def update_kernel(
    subs, nodes, own_ref, weighted_ref, out_ref, landed, sums, node_send, node_recv, sub_send, sub_recv
):
    sub, node = lax.axis_index("sub"), lax.axis_index("node")
    others = [lax.rem(node + k, nodes) for k in range(1, nodes)]
    rest = [lax.rem(sub + k, subs) for k in range(1, subs)]
    meet([{"node": o} for o in others] + [{"sub": o} for o in rest])
    count = own_ref.shape[0]

    def copies(b):
        return [
            remote(
                weighted_ref.at[o, b], landed.at[k, b],
                node_send.at[k, b], node_recv.at[k, b], {"node": o},
            )
            for k, o in enumerate(others)
        ]

    def begin(b, carry):
        for copy in copies(b):
            copy.start()
        return carry

    lax.fori_loop(0, count, begin, 0)

    def step(b, squares):
        for copy in copies(b):
            copy.wait()
        total = own_ref[b] - weighted_ref[node, b]
        for k in range(nodes - 1):
            total = total - landed[k, b]
        out_ref[b] = total
        return squares + jnp.sum(total * total, axis=0, keepdims=True)

    width = own_ref.shape[2]
    squares = lax.fori_loop(0, count, step, jnp.zeros((1, width), jnp.float32))
    sums[sub] = jnp.broadcast_to(squares, (8, width))
    share = [
        remote(sums.at[sub], sums.at[sub], sub_send.at[k], sub_recv.at[k], {"sub": o})
        for k, o in enumerate(rest)
    ]
    for copy in share:
        copy.start()
    for copy in share:
        copy.wait()
    total = sums[0]
    for t in range(1, subs):
        total = total + sums[t]
    rows = count * own_ref.shape[1] * subs
    factor = lax.rsqrt(total / rows + 1e-06)[0:1]

    def scale(b, carry):
        out_ref[b] = out_ref[b] * factor
        return carry

    lax.fori_loop(0, count, scale, 0)


def update_call(own, weighted, subs, nodes):
    count, size, width = own.shape
    return pl.pallas_call(
        functools.partial(update_kernel, subs, nodes),
        out_shape=jax.ShapeDtypeStruct(own.shape, jnp.float32),
        in_specs=[pl.BlockSpec(memory_space=VMEM)] * 2,
        out_specs=pl.BlockSpec(memory_space=VMEM),
        scratch_shapes=[
            VMEM((nodes - 1, count, size, width), jnp.float32),
            VMEM((subs, 8, width), jnp.float32),
            pltpu.SemaphoreType.DMA((nodes - 1, count)),
            pltpu.SemaphoreType.DMA((nodes - 1, count)),
            pltpu.SemaphoreType.DMA((subs - 1,)),
            pltpu.SemaphoreType.DMA((subs - 1,)),
        ],
        compiler_params=pltpu.CompilerParams(collective_id=2, has_side_effects=True),
        name="update",
    )(own, weighted)


def shards(
    search_vectors,
    ritz_values,
    matrix_blocks,
    block_lists,
    inverses,
    panels,
    separator_map,
    separator_shift,
):
    row_count, width = search_vectors.shape
    block_count, _, block_size, _ = matrix_blocks.shape
    nodes, subs = lax.axis_size("node"), lax.axis_size("sub")
    col_count = width // nodes
    node_index = lax.axis_index("node")
    sub_index = lax.axis_index("sub")
    column_start = node_index * col_count
    maps = lax.all_gather(separator_map, "sub", axis=0, tiled=True)
    own_columns = lax.dynamic_slice_in_dim(search_vectors, column_start, col_count, 1)
    own_columns = own_columns.reshape(block_count, block_size, col_count)
    own_ritz = lax.dynamic_slice_in_dim(ritz_values, column_start, col_count, 0)[None, :]
    local_index = block_lists - sub_index * block_count + HALO_BLOCKS
    residual = residual_call(local_index, own_columns, own_ritz, matrix_blocks, subs, nodes)
    residual = residual.transpose(1, 2, 0, 3).reshape(block_count, block_size, width)

    node_local = inverses.shape[0]
    total_nodes = node_local * nodes
    node_ids = (node_index * node_local + jnp.arange(node_local, dtype=jnp.int32)).astype(
        jnp.float32
    )
    angles = math.pi * (node_ids + 0.5) / total_nodes
    real_shift = jnp.cos(angles)
    imag_shift = jnp.sin(angles)
    first_guess = jnp.einsum("ncbij,bjm->ncbim", inverses, residual, precision=HIGH).reshape(
        node_local, 2, row_count, width
    )
    my_panel = panels[0]
    sep_count = my_panel.shape[0] // block_size
    partial_value = jnp.einsum("sr,ncrm->ncsm", my_panel, first_guess, precision=HIGH)
    hits = maps[:, :, None] == jnp.arange(SEP_GROUPS, dtype=jnp.int32)[None, None, :]
    slots = sep_count - jnp.sum(
        hits * (sep_count - jnp.arange(sep_count, dtype=jnp.int32))[None, :, None], axis=1
    )
    picked_back = separator_call(
        maps, slots, separator_shift, real_shift, imag_shift,
        partial_value.reshape(node_local, 2, sep_count, block_size, width), subs,
    ).reshape(node_local, 2, sep_count * block_size, width)
    spread_back = jnp.einsum("sr,ncsm->ncrm", my_panel, picked_back, precision=HIGH).reshape(
        node_local, 2, block_count, block_size, width
    )
    weight_real = (2.0 / total_nodes * real_shift)[:, None, None, None]
    weight_imag = (2.0 / total_nodes * imag_shift)[:, None, None, None]
    by_real = weight_real * inverses[:, 0] - weight_imag * inverses[:, 1]
    by_imag = weight_real * inverses[:, 1] + weight_imag * inverses[:, 0]
    weighted = jnp.zeros((block_count, block_size, width), jnp.float32)
    for n in range(node_local):
        weighted = weighted + jnp.einsum(
            "bij,bjm->bim", by_real[n], residual - spread_back[n, 0], precision=HIGH
        )
        weighted = weighted + jnp.einsum(
            "bij,bjm->bim", by_imag[n], spread_back[n, 1], precision=HIGH
        )
    weighted = weighted.reshape(block_count, block_size, nodes, col_count).transpose(2, 0, 1, 3)
    return update_call(own_columns, weighted, subs, nodes).reshape(row_count, col_count)


def solution(mesh):
    return jax.shard_map(
        shards,
        mesh=mesh,
        in_specs=(
            P("sub", None),
            P(),
            P("sub", None, None, None),
            P("sub", None),
            P("node", None, "sub", None, None),
            P("sub", None, None),
            P("sub", None),
            P(),
        ),
        out_specs=P("sub", "node"),
        check_vma=False,
    )
```

```python
import functools
import math

import jax
import jax.numpy as jnp
from jax import lax
from jax.experimental import pallas as pl
from jax.experimental.pallas import tpu as pltpu
from jax.sharding import PartitionSpec as P

HALO_BLOCKS = 4
SEP_GROUPS = 8
VMEM = pltpu.VMEM
SMEM = pltpu.SMEM


def split(x):
    hi = x.astype(jnp.bfloat16)
    lo = (x - hi.astype(jnp.float32)).astype(jnp.bfloat16)
    return hi, lo


def dot_halves(a, b):
    (a_hi, a_lo), (b_hi, b_lo) = a, b
    dot = functools.partial(jnp.dot, preferred_element_type=jnp.float32)
    return dot(a_hi, b_hi) + (dot(a_hi, b_lo) + dot(a_lo, b_hi))


def dot3(a, b):
    return dot_halves(split(a), split(b))


def meet(targets):
    barrier = pltpu.get_barrier_semaphore()
    for target in targets:
        pl.semaphore_signal(
            barrier, inc=1, device_id=target, device_id_type=pl.DeviceIdType.MESH
        )
    pl.semaphore_wait(barrier, len(targets))


def remote(src, dst, send, recv, target):
    return pltpu.make_async_remote_copy(
        src_ref=src,
        dst_ref=dst,
        send_sem=send,
        recv_sem=recv,
        device_id=target,
        device_id_type=pl.DeviceIdType.MESH,
    )


def inner_size(subs):
    return max(k for k in range(1, subs + 1) if subs % k == 0 and k * k <= subs)


def kernel(
    subs, nodes, inner, cuts, halves,
    index_ref, map_ref, own_ref, ritz_ref, shift_ref, blocks_hbm, inverses_hbm, panel_hbm,
    out_ref, squares_ref,
    blocks, inverses, panel, padded, maps, residual,
    panel_hi, panel_lo, turned_hi, turned_lo, fold_hi, fold_lo, guess_hi, guess_lo,
    part, near, dense, far, coarse, picked, back, weighted, shares, landed, sums,
    load_sem, halo_send, halo_recv, map_send, map_recv, node_send, node_recv,
    sep_send, sep_recv, far_send, far_recv, own_sem,
    share_send, share_recv, sum_send, sum_recv,
):
    sub, node = lax.axis_index("sub"), lax.axis_index("node")
    count, size, _ = own_ref.shape
    node_local = inverses.shape[0]
    total_nodes = node_local * nodes
    outer = subs // inner
    sep_blocks = map_ref.shape[0]
    groups, rows, cols = shift_ref.shape
    span = size // inner
    wide = part.shape[-1]
    width = wide * halves
    place, plane = lax.rem(sub, inner), sub // inner
    base = plane * inner
    near_places = [lax.rem(place + k, inner) for k in range(1, inner)]
    far_planes = [lax.rem(plane + k, outer) for k in range(1, outer)]
    other_nodes = [lax.rem(node + k, nodes) for k in range(1, nodes)]
    other_subs = [lax.rem(sub + k, subs) for k in range(1, subs)]
    after, before = lax.rem(sub + 1, subs), lax.rem(sub + subs - 1, subs)

    loads = [
        pltpu.make_async_copy(panel_hbm, panel, load_sem.at[0]),
        pltpu.make_async_copy(inverses_hbm, inverses, load_sem.at[1]),
        pltpu.make_async_copy(blocks_hbm, blocks, load_sem.at[2]),
        pltpu.make_async_copy(own_ref, padded.at[pl.ds(HALO_BLOCKS, count)], load_sem.at[3]),
        pltpu.make_async_copy(map_ref, maps.at[place], load_sem.at[4]),
    ]
    for load in loads:
        load.start()
    meet([{"sub": o} for o in other_subs] + [{"node": o} for o in other_nodes])
    halo = [
        remote(
            own_ref.at[pl.ds(count - HALO_BLOCKS, HALO_BLOCKS)],
            padded.at[pl.ds(0, HALO_BLOCKS)],
            halo_send.at[0], halo_recv.at[0], {"sub": after},
        ),
        remote(
            own_ref.at[pl.ds(0, HALO_BLOCKS)],
            padded.at[pl.ds(HALO_BLOCKS + count, HALO_BLOCKS)],
            halo_send.at[1], halo_recv.at[1], {"sub": before},
        ),
    ]
    tell = [
        remote(map_ref, maps.at[place], map_send.at[k], map_recv.at[k], {"sub": base + t})
        for k, t in enumerate(near_places)
    ]
    for copy in halo + tell:
        copy.start()

    def constant(values):
        chosen = jnp.float32(values[0])
        for k in range(1, nodes):
            chosen = jnp.where(node == k, jnp.float32(values[k]), chosen)
        return chosen

    angles = [
        [math.pi * (k * node_local + n + 0.5) / total_nodes for k in range(nodes)]
        for n in range(node_local)
    ]
    real_shift = [constant([math.cos(a) for a in row]) for row in angles]
    imag_shift = [constant([math.sin(a) for a in row]) for row in angles]
    real_weight = [constant([2.0 * math.cos(a) / total_nodes for a in row]) for row in angles]
    imag_weight = [constant([2.0 * math.sin(a) / total_nodes for a in row]) for row in angles]

    loads[0].wait()
    for p in range(sep_blocks):
        block = panel[p * size : (p + 1) * size]
        hi, lo = split(block)
        panel_hi[p * size : (p + 1) * size] = hi
        panel_lo[p * size : (p + 1) * size] = lo
        hi, lo = split(block.T)
        turned_hi[:, p * size : (p + 1) * size] = hi
        turned_lo[:, p * size : (p + 1) * size] = lo
    loads[1].wait()
    for n in range(node_local):

        def fold(b, carry):
            real, imag = inverses[n, 0, b], inverses[n, 1, b]
            hi, lo = split(real_weight[n] * real - imag_weight[n] * imag)
            fold_hi[n, b, :, :size], fold_lo[n, b, :, :size] = hi, lo
            hi, lo = split(real_weight[n] * imag + imag_weight[n] * real)
            fold_hi[n, b, :, size:], fold_lo[n, b, :, size:] = hi, lo
            return carry

        lax.fori_loop(0, count, fold, 0)
    for load in loads[2:]:
        load.wait()
    for copy in halo:
        copy.wait()

    def node_copies(b):
        return [
            remote(
                residual.at[node, b], residual.at[node, b],
                node_send.at[k, b], node_recv.at[k, b], {"node": o},
            )
            for k, o in enumerate(other_nodes)
        ]

    def residual_step(b, carry):
        total = -(own_ref[b] * ritz_ref[...])
        for q in range(blocks.shape[1]):
            total = total + dot3(blocks[b, q], padded[index_ref[b, q]])
        residual[node, b] = total
        for copy in node_copies(b):
            copy.start()
        return carry

    lax.fori_loop(0, count, residual_step, 0)

    def whole_residual(b):
        return jnp.concatenate([residual[j, b] for j in range(nodes)], axis=1)

    def guess_step(b, carry):
        for copy in node_copies(b):
            copy.wait()
        right = split(whole_residual(b))
        for n in range(node_local):
            for c in range(2):
                hi, lo = split(dot_halves(split(inverses[n, c, b]), right))
                for h in range(halves):
                    k = n * halves + h
                    chosen = slice(h * wide, (h + 1) * wide)
                    spot = slice(c * wide, (c + 1) * wide)
                    guess_hi[k, b, :, spot] = hi[:, chosen]
                    guess_lo[k, b, :, spot] = lo[:, chosen]
        return carry

    lax.fori_loop(0, count, guess_step, 0)
    for copy in tell:
        copy.wait()

    def strip(ref, t):
        return ref.at[:, :, pl.ds(pl.multiple_of(t * span, span), span)]

    def spot(ref, o):
        row = pl.multiple_of((o // cuts) * rows, rows)
        if cuts == 1:
            return ref.at[:, :, pl.ds(row, rows)]
        col = pl.multiple_of(lax.rem(o, cuts) * cols, cols)
        return ref.at[:, :, pl.ds(row, rows), pl.ds(col, cols)]

    def own_copy(k, src, dst, which):
        return pltpu.make_async_copy(src, dst, own_sem.at[k, which])

    def there_near(k):
        return [
            remote(
                strip(part.at[k], t), near.at[k, place],
                sep_send.at[k, 0, i], sep_recv.at[k, 0, i], {"sub": base + t},
            )
            for i, t in enumerate(near_places)
        ]

    def there_far(k):
        return [
            remote(
                spot(dense.at[k], z), far.at[k, plane],
                far_send.at[k, 0, i], far_recv.at[k, 0, i], {"sub": z * inner + place},
            )
            for i, z in enumerate(far_planes)
        ]

    def home_far(k):
        return [
            remote(
                spot(coarse.at[k], plane), spot(coarse.at[k], plane),
                far_send.at[k, 1, i], far_recv.at[k, 1, i], {"sub": z * inner + place},
            )
            for i, z in enumerate(far_planes)
        ]

    def home_near(k):
        return [
            remote(
                picked.at[k, t], strip(back.at[k], place),
                sep_send.at[k, 1, i], sep_recv.at[k, 1, i], {"sub": base + t},
            )
            for i, t in enumerate(near_places)
        ]

    def begin(copies):
        for copy in copies:
            copy.start()

    def finish(copies):
        for copy in copies:
            copy.wait()

    def stage_a(k):
        rights = (
            guess_hi[k].reshape(count * size, 2 * wide),
            guess_lo[k].reshape(count * size, 2 * wide),
        )
        value = dot_halves((panel_hi[...], panel_lo[...]), rights)
        value = value.reshape(sep_blocks, size, 2 * wide)
        part[k, 0] = value[:, :, :wide]
        part[k, 1] = value[:, :, wide:]
        begin(there_near(k))
        own_copy(k, strip(part.at[k], place), near.at[k, place], 0).start()

    def stage_b(k):
        finish(there_near(k))
        own_copy(k, strip(part.at[k], place), near.at[k, place], 0).wait()

        def group(g, carry):
            number = g.astype(jnp.float32)

            def add(t, totals):
                for p in range(sep_blocks):
                    hit = jnp.broadcast_to(maps[t, p, 0:1], (span, wide)) == number
                    totals = tuple(
                        total + jnp.where(hit, near[k, t, c, p], 0.0)
                        for c, total in enumerate(totals)
                    )
                return totals

            zero = jnp.zeros((span, wide), jnp.float32)
            totals = (zero, zero)
            for t in range(inner):
                totals = add(t, totals)
            dense[k, 0, g], dense[k, 1, g] = totals
            return carry

        lax.fori_loop(0, groups, group, 0)
        begin(there_far(k))
        own_copy(k, spot(dense.at[k], plane), far.at[k, plane], 1).start()

    def stage_c(k):
        finish(there_far(k))
        own_copy(k, spot(dense.at[k], plane), far.at[k, plane], 1).wait()
        n = k // halves
        gap = real_shift[n] - shift_ref[...]
        modulus = gap * gap + imag_shift[n] * imag_shift[n]
        by_real, by_imag = gap / modulus, imag_shift[n] / modulus
        real, imag = far[k, 0, 0], far[k, 0, 1]
        for z in range(1, outer):
            real, imag = real + far[k, z, 0], imag + far[k, z, 1]
        row = pl.multiple_of((plane // cuts) * rows, rows)
        new_real = real * by_real + imag * by_imag
        new_imag = imag * by_real - real * by_imag
        if cuts == 1:
            coarse[k, 0, :, pl.ds(row, rows)] = new_real
            coarse[k, 1, :, pl.ds(row, rows)] = new_imag
        else:
            col = pl.multiple_of(lax.rem(plane, cuts) * cols, cols)
            coarse[k, 0, :, pl.ds(row, rows), pl.ds(col, cols)] = new_real
            coarse[k, 1, :, pl.ds(row, rows), pl.ds(col, cols)] = new_imag
        begin(home_far(k))

    def stage_d(k):
        finish(home_far(k))

        def pick(t, carry):
            for p in range(sep_blocks):
                here = jnp.broadcast_to(maps[t, p, 0:1], (span, wide))
                for c in range(2):
                    value = coarse[k, c, 0]
                    for g in range(1, groups):
                        value = jnp.where(here == float(g), coarse[k, c, g], value)
                    picked[k, t, c, p] = value
            return carry

        lax.fori_loop(0, inner, pick, 0)
        begin(home_near(k))
        own_copy(k, picked.at[k, place], strip(back.at[k], place), 2).start()

    def stage_e(k):
        finish(home_near(k))
        own_copy(k, picked.at[k, place], strip(back.at[k], place), 2).wait()
        n, h = divmod(k, halves)
        right = jnp.concatenate(
            [back[k, c].reshape(sep_blocks * size, wide) for c in range(2)], axis=1
        )
        value = dot_halves((turned_hi[...], turned_lo[...]), split(right))
        value = value.reshape(count, size, 2 * wide)
        for b in range(count):
            chosen = slice(h * wide, (h + 1) * wide)
            lower = jnp.concatenate(
                [whole_residual(b)[:, chosen] - value[b, :, :wide], value[b, :, wide:]], axis=0
            )
            new = dot_halves((fold_hi[n, b], fold_lo[n, b]), split(lower))
            if n > 0:
                new = new + weighted[b, :, chosen]
            weighted[b, :, chosen] = new

    chunks = node_local * halves
    stages = [stage_a, stage_b, stage_c, stage_d, stage_e]
    for k in range(chunks):
        stage_a(k)
    for step in range(1, chunks + len(stages)):
        for s in range(len(stages) - 1, 0, -1):
            k = step - s
            if 0 <= k < chunks:
                stages[s](k)

    part_cols = width // nodes
    for j in range(nodes):
        shares[j] = weighted[:, :, j * part_cols : (j + 1) * part_cols]

    def share_copies(b):
        return [
            remote(
                shares.at[o, b], landed.at[k, b],
                share_send.at[k, b], share_recv.at[k, b], {"node": o},
            )
            for k, o in enumerate(other_nodes)
        ]

    def share_begin(b, carry):
        begin(share_copies(b))
        return carry

    lax.fori_loop(0, count, share_begin, 0)

    def update_step(b, squares):
        finish(share_copies(b))
        total = own_ref[b] - shares[node, b]
        for k in range(nodes - 1):
            total = total - landed[k, b]
        out_ref[b] = total
        return squares + jnp.sum(total * total, axis=0, keepdims=True)

    squares = lax.fori_loop(0, count, update_step, jnp.zeros((1, part_cols), jnp.float32))
    sums[sub] = jnp.broadcast_to(squares, (8, part_cols))
    spread = [
        remote(sums.at[sub], sums.at[sub], sum_send.at[k], sum_recv.at[k], {"sub": o})
        for k, o in enumerate(other_subs)
    ]
    begin(spread)
    finish(spread)
    total = sums[0]
    for t in range(1, subs):
        total = total + sums[t]
    squares_ref[...] = total


def shards(
    search_vectors,
    ritz_values,
    matrix_blocks,
    block_lists,
    inverses,
    panels,
    separator_map,
    separator_shift,
):
    row_count, width = search_vectors.shape
    count, degree, size, _ = matrix_blocks.shape
    nodes, subs = lax.axis_size("node"), lax.axis_size("sub")
    node_local = inverses.shape[0]
    col_count = width // nodes
    sub = lax.axis_index("sub")
    start = lax.axis_index("node") * col_count
    own = lax.dynamic_slice_in_dim(search_vectors, start, col_count, 1)
    own = own.reshape(count, size, col_count)
    own_ritz = lax.dynamic_slice_in_dim(ritz_values, start, col_count, 0)[None, :]
    index = block_lists - sub * count + HALO_BLOCKS

    inner = inner_size(subs)
    outer = subs // inner
    sep_blocks = separator_map.shape[1]
    groups = separator_shift.shape[0] // size
    span = size // inner
    cuts = max(1, outer * 8 // span)
    halves = max(1, width // (size * cuts))
    chunks = node_local * halves
    wide = width // halves
    rows, cols = span * cuts // outer, wide // cuts
    first_row = (sub % inner) * span + (sub // inner // cuts) * rows
    shift = lax.dynamic_slice_in_dim(separator_shift.reshape(groups, size, 1), first_row, rows, 1)
    shift = jnp.broadcast_to(shift, (groups, rows, cols))
    map_tile = jnp.broadcast_to(
        separator_map[0].astype(jnp.float32)[:, None, None], (sep_blocks, 8, wide)
    )
    f32, bf16 = jnp.float32, jnp.bfloat16
    dma = pltpu.SemaphoreType.DMA
    updated, squares = pl.pallas_call(
        functools.partial(kernel, subs, nodes, inner, cuts, halves),
        out_shape=[
            jax.ShapeDtypeStruct(own.shape, f32),
            jax.ShapeDtypeStruct((8, col_count), f32),
        ],
        in_specs=[pl.BlockSpec(memory_space=SMEM)]
        + [pl.BlockSpec(memory_space=VMEM)] * 4
        + [pl.BlockSpec(memory_space=pl.ANY)] * 3,
        out_specs=[pl.BlockSpec(memory_space=VMEM)] * 2,
        scratch_shapes=[
            VMEM(matrix_blocks.shape, f32),
            VMEM(inverses.shape, f32),
            VMEM(panels.shape[1:], f32),
            VMEM((count + 2 * HALO_BLOCKS, size, col_count), f32),
            VMEM((inner, sep_blocks, 8, wide), f32),
            VMEM((nodes, count, size, col_count), f32),
            VMEM(panels.shape[1:], bf16),
            VMEM(panels.shape[1:], bf16),
            VMEM(panels.shape[:0:-1], bf16),
            VMEM(panels.shape[:0:-1], bf16),
            VMEM((node_local, count, size, 2 * size), bf16),
            VMEM((node_local, count, size, 2 * size), bf16),
            VMEM((chunks, count, size, 2 * wide), bf16),
            VMEM((chunks, count, size, 2 * wide), bf16),
            VMEM((chunks, 2, sep_blocks, size, wide), f32),
            VMEM((chunks, inner, 2, sep_blocks, span, wide), f32),
            VMEM((chunks, 2, groups, span, wide), f32),
            VMEM((chunks, outer, 2, groups, rows, cols), f32),
            VMEM((chunks, 2, groups, span, wide), f32),
            VMEM((chunks, inner, 2, sep_blocks, span, wide), f32),
            VMEM((chunks, 2, sep_blocks, size, wide), f32),
            VMEM((count, size, width), f32),
            VMEM((nodes, count, size, col_count), f32),
            VMEM((nodes - 1, count, size, col_count), f32),
            VMEM((subs, 8, col_count), f32),
            dma((5,)),
            dma((2,)),
            dma((2,)),
            dma((inner - 1,)),
            dma((inner - 1,)),
            dma((nodes - 1, count)),
            dma((nodes - 1, count)),
            dma((chunks, 2, inner - 1)),
            dma((chunks, 2, inner - 1)),
            dma((chunks, 2, outer - 1)),
            dma((chunks, 2, outer - 1)),
            dma((chunks, 3)),
            dma((nodes - 1, count)),
            dma((nodes - 1, count)),
            dma((subs - 1,)),
            dma((subs - 1,)),
        ],
        compiler_params=pltpu.CompilerParams(
            collective_id=0, has_side_effects=True, vmem_limit_bytes=60 * 1024 * 1024
        ),
        name="update",
    )(index, map_tile, own, own_ritz, shift, matrix_blocks, inverses, panels[0])
    factor = lax.rsqrt(squares[0:1] / (row_count * subs) + 1e-06)
    return (updated * factor[None]).reshape(row_count, col_count)


def solution(mesh):
    return jax.shard_map(
        shards,
        mesh=mesh,
        in_specs=(
            P("sub", None),
            P(),
            P("sub", None, None, None),
            P("sub", None),
            P("node", None, "sub", None, None),
            P("sub", None, None),
            P("sub", None),
            P(),
        ),
        out_specs=P("sub", "node"),
        check_vma=False,
    )
```

```python
import functools
import math

import jax
import jax.numpy as jnp
from jax import lax
from jax.experimental import pallas as pl
from jax.experimental.pallas import tpu as pltpu
from jax.sharding import PartitionSpec as P

HALO_BLOCKS = 4
SEP_GROUPS = 8
VMEM = pltpu.VMEM
SMEM = pltpu.SMEM


def split(x):
    hi = x.astype(jnp.bfloat16)
    lo = (x - hi.astype(jnp.float32)).astype(jnp.bfloat16)
    return hi, lo


def dot_halves(a, b):
    (a_hi, a_lo), (b_hi, b_lo) = a, b
    dot = functools.partial(jnp.dot, preferred_element_type=jnp.float32)
    return dot(a_hi, b_hi) + (dot(a_hi, b_lo) + dot(a_lo, b_hi))


def dot3(a, b):
    return dot_halves(split(a), split(b))


def meet(targets):
    barrier = pltpu.get_barrier_semaphore()
    for target in targets:
        pl.semaphore_signal(
            barrier, inc=1, device_id=target, device_id_type=pl.DeviceIdType.MESH
        )
    pl.semaphore_wait(barrier, len(targets))


def remote(src, dst, send, recv, target):
    return pltpu.make_async_remote_copy(
        src_ref=src,
        dst_ref=dst,
        send_sem=send,
        recv_sem=recv,
        device_id=target,
        device_id_type=pl.DeviceIdType.MESH,
    )


def inner_size(subs):
    return max(k for k in range(1, subs + 1) if subs % k == 0 and k * k <= subs)


def kernel(
    subs, nodes, inner, halves, sliced,
    index_ref, map_ref, ritz_ref, shift_ref, vectors_hbm, blocks_hbm, inverses_hbm, panel_hbm,
    out_ref, factor_ref,
    own_ref, shift_columns, blocks, inverses, panel, padded, maps, residual,
    panel_hi, panel_lo, turned_hi, turned_lo, fold_hi, fold_lo, guess_hi, guess_lo,
    part, near, dense, far, coarse, picked, back, weighted, shares, landed, sums,
    load_sem, halo_send, halo_recv, map_send, map_recv, node_send, node_recv,
    sep_send, sep_recv, far_send, far_recv, own_sem,
    share_send, share_recv, sum_send, sum_recv,
):
    sub, node = lax.axis_index("sub"), lax.axis_index("node")
    count, size, _ = own_ref.shape
    node_local = inverses.shape[0]
    total_nodes = node_local * nodes
    outer = subs // inner
    sep_blocks = map_ref.shape[1]
    groups = shift_ref.shape[0]
    rounds = far.shape[1]
    span = size // inner
    wide = part.shape[-1]
    width = wide * halves
    place, plane = lax.rem(sub, inner), sub // inner
    base = plane * inner
    near_places = [lax.rem(place + k, inner) for k in range(1, inner)]
    bits = [lax.rem(plane // 2**i, 2) for i in range(rounds)]
    partners = [
        {"sub": (plane + 2**i - 2 * 2**i * bits[i]) * inner + place} for i in range(rounds)
    ]
    other_nodes = [lax.rem(node + k, nodes) for k in range(1, nodes)]
    other_subs = [lax.rem(sub + k, subs) for k in range(1, subs)]
    after, before = lax.rem(sub + 1, subs), lax.rem(sub + subs - 1, subs)

    loads = [
        pltpu.make_async_copy(panel_hbm, panel, load_sem.at[0]),
        pltpu.make_async_copy(inverses_hbm, inverses, load_sem.at[1]),
        pltpu.make_async_copy(blocks_hbm, blocks, load_sem.at[2]),
    ]
    if sliced:
        fetch = vectors_hbm
    else:
        part_cols = vectors_hbm.shape[2] // nodes
        first = pl.multiple_of(node * part_cols, part_cols)
        fetch = vectors_hbm.at[:, :, pl.ds(first, part_cols)]
    fetch = pltpu.make_async_copy(fetch, own_ref, load_sem.at[3])
    fetch.start()
    for load in loads:
        load.start()
    for p in range(sep_blocks):
        value = map_ref[0, p].astype(jnp.float32)
        maps[place, p] = jnp.full(maps.shape[2:], value, jnp.float32)
    ritz_parts = [
        ritz_ref[:, j * own_ref.shape[2] : (j + 1) * own_ref.shape[2]] for j in range(nodes)
    ]
    ritz = ritz_parts[0]
    for j in range(1, nodes):
        ritz = jnp.where(node == j, ritz_parts[j], ritz)
    shift_columns[...] = jnp.concatenate(
        [shift_ref[...], jnp.zeros((size - groups, size), jnp.float32)], axis=0
    ).T
    fetch.wait()
    meet([{"sub": o} for o in other_subs] + [{"node": o} for o in other_nodes])
    halo = [
        remote(
            own_ref.at[pl.ds(count - HALO_BLOCKS, HALO_BLOCKS)],
            padded.at[pl.ds(0, HALO_BLOCKS)],
            halo_send.at[0], halo_recv.at[0], {"sub": after},
        ),
        remote(
            own_ref.at[pl.ds(0, HALO_BLOCKS)],
            padded.at[pl.ds(HALO_BLOCKS + count, HALO_BLOCKS)],
            halo_send.at[1], halo_recv.at[1], {"sub": before},
        ),
    ]
    tell = [
        remote(maps.at[place], maps.at[place], map_send.at[k], map_recv.at[k], {"sub": base + t})
        for k, t in enumerate(near_places)
    ]
    for copy in halo + tell:
        copy.start()

    def constant(values):
        chosen = jnp.float32(values[0])
        for k in range(1, nodes):
            chosen = jnp.where(node == k, jnp.float32(values[k]), chosen)
        return chosen

    angles = [
        [math.pi * (k * node_local + n + 0.5) / total_nodes for k in range(nodes)]
        for n in range(node_local)
    ]
    real_shift = [constant([math.cos(a) for a in row]) for row in angles]
    imag_shift = [constant([math.sin(a) for a in row]) for row in angles]
    real_weight = [constant([2.0 * math.cos(a) / total_nodes for a in row]) for row in angles]
    imag_weight = [constant([2.0 * math.sin(a) / total_nodes for a in row]) for row in angles]

    loads[0].wait()
    for p in range(sep_blocks):
        block = panel[p * size : (p + 1) * size]
        hi, lo = split(block)
        panel_hi[p * size : (p + 1) * size] = hi
        panel_lo[p * size : (p + 1) * size] = lo
        hi, lo = split(block.T)
        turned_hi[:, p * size : (p + 1) * size] = hi
        turned_lo[:, p * size : (p + 1) * size] = lo
    loads[1].wait()
    for n in range(node_local):

        def fold(b, carry):
            real, imag = inverses[n, 0, b], inverses[n, 1, b]
            hi, lo = split(real_weight[n] * real - imag_weight[n] * imag)
            fold_hi[n, b, :, :size], fold_lo[n, b, :, :size] = hi, lo
            hi, lo = split(real_weight[n] * imag + imag_weight[n] * real)
            fold_hi[n, b, :, size:], fold_lo[n, b, :, size:] = hi, lo
            return carry

        lax.fori_loop(0, count, fold, 0)
    loads[2].wait()

    def diagonal(b, carry):
        out_ref[b] = dot3(blocks[b, 0], own_ref[b]) - own_ref[b] * ritz
        return carry

    lax.fori_loop(0, count, diagonal, 0)
    place_own = pltpu.make_async_copy(
        own_ref, padded.at[pl.ds(HALO_BLOCKS, count)], load_sem.at[4]
    )
    place_own.start()
    place_own.wait()
    for copy in halo:
        copy.wait()

    def node_copies(b):
        return [
            remote(
                residual.at[node, b], residual.at[node, b],
                node_send.at[k, b], node_recv.at[k, b], {"node": o},
            )
            for k, o in enumerate(other_nodes)
        ]

    def residual_step(b, carry):
        total = out_ref[b]
        for q in range(1, blocks.shape[1]):
            spot = index_ref[b, q] - sub * count + HALO_BLOCKS
            spot = jnp.clip(spot, 0, padded.shape[0] - 1)
            total = total + dot3(blocks[b, q], padded[spot])
        residual[node, b] = total
        for copy in node_copies(b):
            copy.start()
        return carry

    lax.fori_loop(0, count, residual_step, 0)

    def whole_residual(b):
        return jnp.concatenate([residual[j, b] for j in range(nodes)], axis=1)

    def guess(n):
        def step(b, carry):
            if n == 0:
                for copy in node_copies(b):
                    copy.wait()
            right = split(whole_residual(b))
            for c in range(2):
                hi, lo = split(dot_halves(split(inverses[n, c, b]), right))
                for h in range(halves):
                    k = n * halves + h
                    chosen = slice(h * wide, (h + 1) * wide)
                    spot = slice(c * wide, (c + 1) * wide)
                    guess_hi[k, b, :, spot] = hi[:, chosen]
                    guess_lo[k, b, :, spot] = lo[:, chosen]
            return carry

        lax.fori_loop(0, count, step, 0)

    for copy in tell:
        copy.wait()

    def strip(ref, t):
        return ref.at[:, :, pl.ds(pl.multiple_of(t * span, span), span)]

    def region(level, other=False):
        row, col, row_size, col_size = 0, 0, span, wide
        for i in range(level):
            bit = 1 - bits[i] if other and i == level - 1 else bits[i]
            if row_size >= 16:
                row_size //= 2
                row = row + bit * row_size
            else:
                col_size //= 2
                col = col + bit * col_size
        if not isinstance(row, int):
            row = pl.multiple_of(row, 8)
        if not isinstance(col, int):
            col = pl.multiple_of(col, 128)
        return pl.ds(row, row_size), pl.ds(col, col_size)

    def corner(level):
        row, col = region(level)
        return pl.ds(0, row.size), pl.ds(0, col.size)

    def own_copy(k, src, dst, which):
        return pltpu.make_async_copy(src, dst, own_sem.at[k, which])

    def there_near(k):
        return [
            remote(
                strip(part.at[k], t), near.at[k, place],
                sep_send.at[k, 0, i], sep_recv.at[k, 0, i], {"sub": base + t},
            )
            for i, t in enumerate(near_places)
        ]

    def there_far(k, i):
        return [
            remote(
                dense.at[(k, slice(None), slice(None)) + region(i + 1, True)],
                far.at[(k, i, slice(None), slice(None)) + corner(i + 1)],
                far_send.at[k, 0, i], far_recv.at[k, 0, i], partners[i],
            )
        ]

    def home_far(k, i):
        mine = (k, slice(None), slice(None)) + region(i + 1)
        return [
            remote(
                coarse.at[mine], coarse.at[mine],
                far_send.at[k, 1, i], far_recv.at[k, 1, i], partners[i],
            )
        ]

    def home_near(k):
        return [
            remote(
                picked.at[k, t], strip(back.at[k], place),
                sep_send.at[k, 1, i], sep_recv.at[k, 1, i], {"sub": base + t},
            )
            for i, t in enumerate(near_places)
        ]

    def begin(copies):
        for copy in copies:
            copy.start()

    def finish(copies):
        for copy in copies:
            copy.wait()

    def stage_a(k):
        rights = (
            guess_hi[k].reshape(count * size, 2 * wide),
            guess_lo[k].reshape(count * size, 2 * wide),
        )
        value = dot_halves((panel_hi[...], panel_lo[...]), rights)
        value = value.reshape(sep_blocks, size, 2 * wide)
        part[k, 0] = value[:, :, :wide]
        part[k, 1] = value[:, :, wide:]
        begin(there_near(k))
        own_copy(k, strip(part.at[k], place), near.at[k, place], 0).start()

    def stage_b(k):
        finish(there_near(k))
        own_copy(k, strip(part.at[k], place), near.at[k, place], 0).wait()

        def group(g, carry):
            number = g.astype(jnp.float32)

            def add(t, totals):
                for p in range(sep_blocks):
                    hit = jnp.broadcast_to(maps[t, p, 0:1], (span, wide)) == number
                    totals = tuple(
                        total + jnp.where(hit, near[k, t, c, p], 0.0)
                        for c, total in enumerate(totals)
                    )
                return totals

            zero = jnp.zeros((span, wide), jnp.float32)
            totals = (zero, zero)
            for t in range(inner):
                totals = add(t, totals)
            dense[k, 0, g], dense[k, 1, g] = totals
            return carry

        lax.fori_loop(0, groups, group, 0)
        begin(there_far(k, 0))

    def stage_c(k, i):
        finish(there_far(k, i))
        mine = (k, slice(None), slice(None)) + region(i + 1)
        value = dense[mine] + far[(k, i, slice(None), slice(None)) + corner(i + 1)]
        if i < rounds - 1:
            dense[mine] = value
            begin(there_far(k, i + 1))
            return
        n = k // halves
        row, col = region(rounds)
        first = pl.multiple_of(place * span + row.start, 8)
        columns = shift_columns[pl.ds(first, row.size)]
        for g in range(groups):
            gap = real_shift[n] - columns[:, g : g + 1]
            modulus = gap * gap + imag_shift[n] * imag_shift[n]
            shape = (row.size, col.size)
            by_real = jnp.broadcast_to(gap / modulus, shape)
            by_imag = jnp.broadcast_to(imag_shift[n] / modulus, shape)
            real, imag = value[0, g], value[1, g]
            coarse[k, 0, g, row, col] = real * by_real + imag * by_imag
            coarse[k, 1, g, row, col] = imag * by_real - real * by_imag
        begin(home_far(k, rounds - 1))

    def stage_h(k, i):
        finish(home_far(k, i))
        begin(home_far(k, i - 1))

    def stage_d(k):
        finish(home_far(k, 0))

        def pick(t, carry):
            for p in range(sep_blocks):
                here = jnp.broadcast_to(maps[t, p, 0:1], (span, wide))
                for c in range(2):
                    value = coarse[k, c, 0]
                    for g in range(1, groups):
                        value = jnp.where(here == float(g), coarse[k, c, g], value)
                    picked[k, t, c, p] = value
            return carry

        lax.fori_loop(0, inner, pick, 0)
        begin(home_near(k))
        own_copy(k, picked.at[k, place], strip(back.at[k], place), 2).start()

    def stage_e(k):
        finish(home_near(k))
        own_copy(k, picked.at[k, place], strip(back.at[k], place), 2).wait()
        n, h = divmod(k, halves)
        right = jnp.concatenate(
            [back[k, c].reshape(sep_blocks * size, wide) for c in range(2)], axis=1
        )
        value = dot_halves((turned_hi[...], turned_lo[...]), split(right))
        value = value.reshape(count, size, 2 * wide)
        for b in range(count):
            chosen = slice(h * wide, (h + 1) * wide)
            lower = jnp.concatenate(
                [whole_residual(b)[:, chosen] - value[b, :, :wide], value[b, :, wide:]], axis=0
            )
            new = dot_halves((fold_hi[n, b], fold_lo[n, b]), split(lower))
            if n > 0:
                new = new + weighted[b, :, chosen]
            weighted[b, :, chosen] = new

    chunks = node_local * halves
    stages = [stage_b]
    stages += [functools.partial(stage_c, i=i) for i in range(rounds)]
    stages += [functools.partial(stage_h, i=i) for i in range(rounds - 1, 0, -1)]
    stages += [stage_d, stage_e]
    for n in range(node_local):
        guess(n)
        for h in range(halves):
            stage_a(n * halves + h)
    for step in range(chunks + len(stages) - 1):
        for s, stage in enumerate(stages):
            if 0 <= step - s < chunks:
                stage(step - s)

    part_cols = width // nodes
    for j in range(nodes):
        shares[j] = weighted[:, :, j * part_cols : (j + 1) * part_cols]

    def share_copies(b):
        return [
            remote(
                shares.at[o, b], landed.at[k, b],
                share_send.at[k, b], share_recv.at[k, b], {"node": o},
            )
            for k, o in enumerate(other_nodes)
        ]

    def share_begin(b, carry):
        begin(share_copies(b))
        return carry

    lax.fori_loop(0, count, share_begin, 0)

    def update_step(b, squares):
        finish(share_copies(b))
        total = own_ref[b] - shares[node, b]
        for k in range(nodes - 1):
            total = total - landed[k, b]
        out_ref[b] = total
        return squares + jnp.sum(total * total, axis=0, keepdims=True)

    squares = lax.fori_loop(0, count, update_step, jnp.zeros((1, part_cols), jnp.float32))
    sums[sub] = jnp.broadcast_to(squares, (8, part_cols))
    spread = [
        remote(sums.at[sub], sums.at[sub], sum_send.at[k], sum_recv.at[k], {"sub": o})
        for k, o in enumerate(other_subs)
    ]
    begin(spread)
    finish(spread)
    total = sums[0]
    for t in range(1, subs):
        total = total + sums[t]
    rows = count * size * subs
    factor_ref[...] = lax.rsqrt(total / rows + 1e-06)


def shards(
    search_vectors,
    ritz_values,
    matrix_blocks,
    block_lists,
    inverses,
    panels,
    separator_map,
    separator_shift,
):
    row_count, width = search_vectors.shape
    count, degree, size, _ = matrix_blocks.shape
    nodes, subs = lax.axis_size("node"), lax.axis_size("sub")
    node_local = inverses.shape[0]
    col_count = width // nodes
    vectors = search_vectors
    sliced = col_count % 128 != 0
    if sliced:
        start = lax.axis_index("node") * col_count
        vectors = lax.dynamic_slice_in_dim(vectors, start, col_count, 1)
    vectors = vectors.reshape(count, size, -1)

    inner = inner_size(subs)
    outer = subs // inner
    sep_blocks = separator_map.shape[1]
    groups = separator_shift.shape[0] // size
    span = size // inner
    rounds = max(1, (outer - 1).bit_length())
    halves = width // size if span // outer >= 8 else 1
    chunks = node_local * halves
    wide = width // halves
    f32, bf16 = jnp.float32, jnp.bfloat16
    dma = pltpu.SemaphoreType.DMA
    updated, factor = pl.pallas_call(
        functools.partial(kernel, subs, nodes, inner, halves, sliced),
        out_shape=[
            jax.ShapeDtypeStruct((count, size, col_count), f32),
            jax.ShapeDtypeStruct((8, col_count), f32),
        ],
        in_specs=[pl.BlockSpec(memory_space=SMEM)] * 2
        + [pl.BlockSpec(memory_space=VMEM)] * 2
        + [pl.BlockSpec(memory_space=pl.ANY)] * 4,
        out_specs=[pl.BlockSpec(memory_space=VMEM)] * 2,
        scratch_shapes=[
            VMEM((count, size, col_count), f32),
            VMEM((size, size), f32),
            VMEM(matrix_blocks.shape, f32),
            VMEM(inverses.shape, f32),
            VMEM(panels.shape[1:], f32),
            VMEM((count + 2 * HALO_BLOCKS, size, col_count), f32),
            VMEM((inner, sep_blocks, 8, wide), f32),
            VMEM((nodes, count, size, col_count), f32),
            VMEM(panels.shape[1:], bf16),
            VMEM(panels.shape[1:], bf16),
            VMEM(panels.shape[:0:-1], bf16),
            VMEM(panels.shape[:0:-1], bf16),
            VMEM((node_local, count, size, 2 * size), bf16),
            VMEM((node_local, count, size, 2 * size), bf16),
            VMEM((chunks, count, size, 2 * wide), bf16),
            VMEM((chunks, count, size, 2 * wide), bf16),
            VMEM((chunks, 2, sep_blocks, size, wide), f32),
            VMEM((chunks, inner, 2, sep_blocks, span, wide), f32),
            VMEM((chunks, 2, groups, span, wide), f32),
            VMEM((chunks, rounds, 2, groups, span // 2, wide), f32),
            VMEM((chunks, 2, groups, span, wide), f32),
            VMEM((chunks, inner, 2, sep_blocks, span, wide), f32),
            VMEM((chunks, 2, sep_blocks, size, wide), f32),
            VMEM((count, size, width), f32),
            VMEM((nodes, count, size, col_count), f32),
            VMEM((nodes - 1, count, size, col_count), f32),
            VMEM((subs, 8, col_count), f32),
            dma((5,)),
            dma((2,)),
            dma((2,)),
            dma((inner - 1,)),
            dma((inner - 1,)),
            dma((nodes - 1, count)),
            dma((nodes - 1, count)),
            dma((chunks, 2, inner - 1)),
            dma((chunks, 2, inner - 1)),
            dma((chunks, 2, rounds)),
            dma((chunks, 2, rounds)),
            dma((chunks, 3)),
            dma((nodes - 1, count)),
            dma((nodes - 1, count)),
            dma((subs - 1,)),
            dma((subs - 1,)),
        ],
        compiler_params=pltpu.CompilerParams(
            collective_id=0, has_side_effects=True, vmem_limit_bytes=60 * 1024 * 1024
        ),
        name="update",
    )(
        block_lists, separator_map, ritz_values[None], separator_shift.reshape(groups, size),
        vectors, matrix_blocks, inverses, panels[0],
    )
    return (updated * factor[None, 0:1]).reshape(row_count, col_count)


def solution(mesh):
    return jax.shard_map(
        shards,
        mesh=mesh,
        in_specs=(
            P("sub", None),
            P(),
            P("sub", None, None, None),
            P("sub", None),
            P("node", None, "sub", None, None),
            P("sub", None, None),
            P("sub", None),
            P(),
        ),
        out_specs=P("sub", "node"),
        check_vma=False,
    )
```

```python
import functools
import math

import jax
import jax.numpy as jnp
from jax import lax
from jax.experimental import pallas as pl
from jax.experimental.pallas import tpu as pltpu
from jax.sharding import PartitionSpec as P

HALO_BLOCKS = 4
SEP_GROUPS = 8
VMEM = pltpu.VMEM
SMEM = pltpu.SMEM


def split(x):
    hi = x.astype(jnp.bfloat16)
    lo = (x - hi.astype(jnp.float32)).astype(jnp.bfloat16)
    return hi, lo


def dot_halves(a, b):
    (a_hi, a_lo), (b_hi, b_lo) = a, b
    dot = functools.partial(jnp.dot, preferred_element_type=jnp.float32)
    return dot(a_hi, b_hi) + (dot(a_hi, b_lo) + dot(a_lo, b_hi))


def dot3(a, b):
    return dot_halves(split(a), split(b))


def meet(targets):
    barrier = pltpu.get_barrier_semaphore()
    for target in targets:
        pl.semaphore_signal(
            barrier, inc=1, device_id=target, device_id_type=pl.DeviceIdType.MESH
        )
    pl.semaphore_wait(barrier, len(targets))


def remote(src, dst, send, recv, target):
    return pltpu.make_async_remote_copy(
        src_ref=src,
        dst_ref=dst,
        send_sem=send,
        recv_sem=recv,
        device_id=target,
        device_id_type=pl.DeviceIdType.MESH,
    )


def inner_size(subs):
    return max(k for k in range(1, subs + 1) if subs % k == 0 and k * k <= subs)


def kernel(
    subs, nodes, inner, halves, sliced,
    index_ref, map_ref, ritz_ref, shift_ref, vectors_hbm, blocks_hbm, inverses_hbm, panel_hbm,
    out_ref, factor_ref,
    own_ref, shift_columns, blocks, inverses, panel, padded, maps, residual,
    panel_hi, panel_lo, turned_hi, turned_lo, fold_hi, fold_lo, guess_hi, guess_lo,
    part, near, dense, far, coarse, picked, back, weighted, shares, landed, sums,
    load_sem, halo_send, halo_recv, map_send, map_recv, node_send, node_recv,
    sep_send, sep_recv, far_send, far_recv, own_sem,
    share_send, share_recv, sum_send, sum_recv,
):
    sub, node = lax.axis_index("sub"), lax.axis_index("node")
    count, size, _ = own_ref.shape
    node_local = inverses.shape[0]
    total_nodes = node_local * nodes
    outer = subs // inner
    sep_blocks = map_ref.shape[1]
    groups = shift_ref.shape[0]
    rounds = far.shape[1]
    span = size // inner
    wide = part.shape[-1]
    width = wide * halves
    place, plane = lax.rem(sub, inner), sub // inner
    base = plane * inner
    near_places = [lax.rem(place + k, inner) for k in range(1, inner)]
    bits = [lax.rem(plane // 2**i, 2) for i in range(rounds)]
    partners = [
        {"sub": (plane + 2**i - 2 * 2**i * bits[i]) * inner + place} for i in range(rounds)
    ]
    other_nodes = [lax.rem(node + k, nodes) for k in range(1, nodes)]
    other_subs = [lax.rem(sub + k, subs) for k in range(1, subs)]
    after, before = lax.rem(sub + 1, subs), lax.rem(sub + subs - 1, subs)

    loads = [
        pltpu.make_async_copy(panel_hbm, panel, load_sem.at[0]),
        pltpu.make_async_copy(inverses_hbm, inverses, load_sem.at[1]),
        pltpu.make_async_copy(blocks_hbm, blocks, load_sem.at[2]),
    ]
    if sliced:
        fetch = vectors_hbm
    else:
        part_cols = vectors_hbm.shape[2] // nodes
        first = pl.multiple_of(node * part_cols, part_cols)
        fetch = vectors_hbm.at[:, :, pl.ds(first, part_cols)]
    fetch = pltpu.make_async_copy(fetch, own_ref, load_sem.at[3])
    fetch.start()
    for load in loads:
        load.start()
    for p in range(sep_blocks):
        value = map_ref[0, p].astype(jnp.float32)
        maps[place, p] = jnp.full(maps.shape[2:], value, jnp.float32)
    ritz_parts = [
        ritz_ref[:, j * own_ref.shape[2] : (j + 1) * own_ref.shape[2]] for j in range(nodes)
    ]
    ritz = ritz_parts[0]
    for j in range(1, nodes):
        ritz = jnp.where(node == j, ritz_parts[j], ritz)
    shift_columns[...] = jnp.concatenate(
        [shift_ref[...], jnp.zeros((size - groups, size), jnp.float32)], axis=0
    ).T
    fetch.wait()
    meet([{"sub": o} for o in other_subs] + [{"node": o} for o in other_nodes])
    halo = [
        remote(
            own_ref.at[pl.ds(count - HALO_BLOCKS, HALO_BLOCKS)],
            padded.at[pl.ds(0, HALO_BLOCKS)],
            halo_send.at[0], halo_recv.at[0], {"sub": after},
        ),
        remote(
            own_ref.at[pl.ds(0, HALO_BLOCKS)],
            padded.at[pl.ds(HALO_BLOCKS + count, HALO_BLOCKS)],
            halo_send.at[1], halo_recv.at[1], {"sub": before},
        ),
    ]
    tell = [
        remote(maps.at[place], maps.at[place], map_send.at[k], map_recv.at[k], {"sub": base + t})
        for k, t in enumerate(near_places)
    ]
    for copy in halo + tell:
        copy.start()

    def constant(values):
        chosen = jnp.float32(values[0])
        for k in range(1, nodes):
            chosen = jnp.where(node == k, jnp.float32(values[k]), chosen)
        return chosen

    angles = [
        [math.pi * (k * node_local + n + 0.5) / total_nodes for k in range(nodes)]
        for n in range(node_local)
    ]
    real_shift = [constant([math.cos(a) for a in row]) for row in angles]
    imag_shift = [constant([math.sin(a) for a in row]) for row in angles]
    real_weight = [constant([2.0 * math.cos(a) / total_nodes for a in row]) for row in angles]
    imag_weight = [constant([2.0 * math.sin(a) / total_nodes for a in row]) for row in angles]

    loads[0].wait()
    for p in range(sep_blocks):
        block = panel[p * size : (p + 1) * size]
        hi, lo = split(block)
        panel_hi[p * size : (p + 1) * size] = hi
        panel_lo[p * size : (p + 1) * size] = lo
    loads[1].wait()
    for n in range(node_local):

        def fold(b, carry):
            real, imag = inverses[n, 0, b], inverses[n, 1, b]
            hi, lo = split(real_weight[n] * real - imag_weight[n] * imag)
            fold_hi[n, b, :, :size], fold_lo[n, b, :, :size] = hi, lo
            hi, lo = split(real_weight[n] * imag + imag_weight[n] * real)
            fold_hi[n, b, :, size:], fold_lo[n, b, :, size:] = hi, lo
            return carry

        lax.fori_loop(0, count, fold, 0)
    loads[2].wait()

    def diagonal(b, carry):
        out_ref[b] = dot3(blocks[b, 0], own_ref[b]) - own_ref[b] * ritz
        return carry

    lax.fori_loop(0, count, diagonal, 0)
    place_own = pltpu.make_async_copy(
        own_ref, padded.at[pl.ds(HALO_BLOCKS, count)], load_sem.at[4]
    )
    place_own.start()
    place_own.wait()
    for copy in halo:
        copy.wait()

    def node_copies(b):
        return [
            remote(
                residual.at[node, b], residual.at[node, b],
                node_send.at[k, b], node_recv.at[k, b], {"node": o},
            )
            for k, o in enumerate(other_nodes)
        ]

    def residual_step(b, carry):
        total = out_ref[b]
        for q in range(1, blocks.shape[1]):
            spot = index_ref[b, q] - sub * count + HALO_BLOCKS
            spot = jnp.clip(spot, 0, padded.shape[0] - 1)
            total = total + dot3(blocks[b, q], padded[spot])
        residual[node, b] = total
        for copy in node_copies(b):
            copy.start()
        return carry

    lax.fori_loop(0, count, residual_step, 0)

    def whole_residual(b):
        return jnp.concatenate([residual[j, b] for j in range(nodes)], axis=1)

    def guess(n):
        def step(b, carry):
            if n == 0:
                for copy in node_copies(b):
                    copy.wait()
            right = split(whole_residual(b))
            for c in range(2):
                hi, lo = split(dot_halves(split(inverses[n, c, b]), right))
                for h in range(halves):
                    k = n * halves + h
                    chosen = slice(h * wide, (h + 1) * wide)
                    spot = slice(c * wide, (c + 1) * wide)
                    guess_hi[k, b, :, spot] = hi[:, chosen]
                    guess_lo[k, b, :, spot] = lo[:, chosen]
            return carry

        lax.fori_loop(0, count, step, 0)

    for copy in tell:
        copy.wait()

    def strip(ref, t):
        return ref.at[:, :, pl.ds(pl.multiple_of(t * span, span), span)]

    def region(level, other=False):
        row, col, row_size, col_size = 0, 0, span, wide
        for i in range(level):
            bit = 1 - bits[i] if other and i == level - 1 else bits[i]
            if row_size >= 16:
                row_size //= 2
                row = row + bit * row_size
            else:
                col_size //= 2
                col = col + bit * col_size
        if not isinstance(row, int):
            row = pl.multiple_of(row, 8)
        if not isinstance(col, int):
            col = pl.multiple_of(col, 128)
        return pl.ds(row, row_size), pl.ds(col, col_size)

    def corner(level):
        row, col = region(level)
        return pl.ds(0, row.size), pl.ds(0, col.size)

    def own_copy(k, src, dst, which):
        return pltpu.make_async_copy(src, dst, own_sem.at[k, which])

    def there_near(k):
        return [
            remote(
                strip(part.at[k], t), near.at[k, place],
                sep_send.at[k, 0, i], sep_recv.at[k, 0, i], {"sub": base + t},
            )
            for i, t in enumerate(near_places)
        ]

    def there_far(k, i):
        return [
            remote(
                dense.at[(k, slice(None), slice(None)) + region(i + 1, True)],
                far.at[(k, i, slice(None), slice(None)) + corner(i + 1)],
                far_send.at[k, 0, i], far_recv.at[k, 0, i], partners[i],
            )
        ]

    def home_far(k, i):
        mine = (k, slice(None), slice(None)) + region(i + 1)
        return [
            remote(
                coarse.at[mine], coarse.at[mine],
                far_send.at[k, 1, i], far_recv.at[k, 1, i], partners[i],
            )
        ]

    def home_near(k):
        return [
            remote(
                picked.at[k, t], strip(back.at[k], place),
                sep_send.at[k, 1, i], sep_recv.at[k, 1, i], {"sub": base + t},
            )
            for i, t in enumerate(near_places)
        ]

    def begin(copies):
        for copy in copies:
            copy.start()

    def finish(copies):
        for copy in copies:
            copy.wait()

    def stage_a(k):
        rights = (
            guess_hi[k].reshape(count * size, 2 * wide),
            guess_lo[k].reshape(count * size, 2 * wide),
        )
        value = dot_halves((panel_hi[...], panel_lo[...]), rights)
        value = value.reshape(sep_blocks, size, 2 * wide)
        part[k, 0] = value[:, :, :wide]
        part[k, 1] = value[:, :, wide:]
        begin(there_near(k))
        own_copy(k, strip(part.at[k], place), near.at[k, place], 0).start()

    def stage_b(k):
        finish(there_near(k))
        own_copy(k, strip(part.at[k], place), near.at[k, place], 0).wait()

        def group(g, carry):
            number = g.astype(jnp.float32)

            def add(t, totals):
                for p in range(sep_blocks):
                    hit = jnp.broadcast_to(maps[t, p, 0:1], (span, wide)) == number
                    totals = tuple(
                        total + jnp.where(hit, near[k, t, c, p], 0.0)
                        for c, total in enumerate(totals)
                    )
                return totals

            zero = jnp.zeros((span, wide), jnp.float32)
            totals = (zero, zero)
            for t in range(inner):
                totals = add(t, totals)
            dense[k, 0, g], dense[k, 1, g] = totals
            return carry

        lax.fori_loop(0, groups, group, 0)
        begin(there_far(k, 0))

    def stage_c(k, i):
        finish(there_far(k, i))
        mine = (k, slice(None), slice(None)) + region(i + 1)
        value = dense[mine] + far[(k, i, slice(None), slice(None)) + corner(i + 1)]
        if i < rounds - 1:
            dense[mine] = value
            begin(there_far(k, i + 1))
            return
        n = k // halves
        row, col = region(rounds)
        first = pl.multiple_of(place * span + row.start, 8)
        columns = shift_columns[pl.ds(first, row.size)]
        for g in range(groups):
            gap = real_shift[n] - columns[:, g : g + 1]
            modulus = gap * gap + imag_shift[n] * imag_shift[n]
            shape = (row.size, col.size)
            by_real = jnp.broadcast_to(gap / modulus, shape)
            by_imag = jnp.broadcast_to(imag_shift[n] / modulus, shape)
            real, imag = value[0, g], value[1, g]
            coarse[k, 0, g, row, col] = real * by_real + imag * by_imag
            coarse[k, 1, g, row, col] = imag * by_real - real * by_imag
        begin(home_far(k, rounds - 1))

    def stage_h(k, i):
        finish(home_far(k, i))
        begin(home_far(k, i - 1))

    def stage_d(k):
        finish(home_far(k, 0))

        def pick(t, carry):
            for p in range(sep_blocks):
                here = jnp.broadcast_to(maps[t, p, 0:1], (span, wide))
                for c in range(2):
                    value = coarse[k, c, 0]
                    for g in range(1, groups):
                        value = jnp.where(here == float(g), coarse[k, c, g], value)
                    picked[k, t, c, p] = value
            return carry

        lax.fori_loop(0, inner, pick, 0)
        begin(home_near(k))
        own_copy(k, picked.at[k, place], strip(back.at[k], place), 2).start()

    def stage_e(k):
        finish(home_near(k))
        own_copy(k, picked.at[k, place], strip(back.at[k], place), 2).wait()
        n, h = divmod(k, halves)
        right = jnp.concatenate(
            [back[k, c].reshape(sep_blocks * size, wide) for c in range(2)], axis=1
        )
        value = dot_halves((turned_hi[...], turned_lo[...]), split(right))
        value = value.reshape(count, size, 2 * wide)
        for b in range(count):
            chosen = slice(h * wide, (h + 1) * wide)
            lower = jnp.concatenate(
                [whole_residual(b)[:, chosen] - value[b, :, :wide], value[b, :, wide:]], axis=0
            )
            new = dot_halves((fold_hi[n, b], fold_lo[n, b]), split(lower))
            if n > 0:
                new = new + weighted[b, :, chosen]
            weighted[b, :, chosen] = new

    def turn(p):
        hi, lo = split(panel[p * size : (p + 1) * size].T)
        turned_hi[:, p * size : (p + 1) * size] = hi
        turned_lo[:, p * size : (p + 1) * size] = lo

    chunks = node_local * halves
    stages = [stage_b]
    stages += [functools.partial(stage_c, i=i) for i in range(rounds)]
    stages += [functools.partial(stage_h, i=i) for i in range(rounds - 1, 0, -1)]
    stages += [stage_d, stage_e]
    for n in range(node_local):
        guess(n)
        for h in range(halves):
            stage_a(n * halves + h)
    for step in range(chunks + len(stages) - 1):
        for s, stage in enumerate(stages):
            if 0 <= step - s < chunks:
                stage(step - s)
        for p in range(sep_blocks):
            if p % (len(stages) - 2) == step:
                turn(p)

    part_cols = width // nodes
    for j in range(nodes):
        shares[j] = weighted[:, :, j * part_cols : (j + 1) * part_cols]

    def share_copies(b):
        return [
            remote(
                shares.at[o, b], landed.at[k, b],
                share_send.at[k, b], share_recv.at[k, b], {"node": o},
            )
            for k, o in enumerate(other_nodes)
        ]

    def share_begin(b, carry):
        begin(share_copies(b))
        return carry

    lax.fori_loop(0, count, share_begin, 0)

    def update_step(b, squares):
        finish(share_copies(b))
        total = own_ref[b] - shares[node, b]
        for k in range(nodes - 1):
            total = total - landed[k, b]
        out_ref[b] = total
        return squares + jnp.sum(total * total, axis=0, keepdims=True)

    squares = lax.fori_loop(0, count, update_step, jnp.zeros((1, part_cols), jnp.float32))
    sums[sub] = jnp.broadcast_to(squares, (8, part_cols))
    spread = [
        remote(sums.at[sub], sums.at[sub], sum_send.at[k], sum_recv.at[k], {"sub": o})
        for k, o in enumerate(other_subs)
    ]
    begin(spread)
    finish(spread)
    total = sums[0]
    for t in range(1, subs):
        total = total + sums[t]
    rows = count * size * subs
    factor_ref[...] = lax.rsqrt(total[0:1] / rows + 1e-06)


def shards(
    search_vectors,
    ritz_values,
    matrix_blocks,
    block_lists,
    inverses,
    panels,
    separator_map,
    separator_shift,
):
    row_count, width = search_vectors.shape
    count, degree, size, _ = matrix_blocks.shape
    nodes, subs = lax.axis_size("node"), lax.axis_size("sub")
    node_local = inverses.shape[0]
    col_count = width // nodes
    vectors = search_vectors
    sliced = col_count % 128 != 0
    if sliced:
        start = lax.axis_index("node") * col_count
        vectors = lax.dynamic_slice_in_dim(vectors, start, col_count, 1)
    vectors = vectors.reshape(count, size, -1)

    inner = inner_size(subs)
    outer = subs // inner
    sep_blocks = separator_map.shape[1]
    groups = separator_shift.shape[0] // size
    span = size // inner
    rounds = max(1, (outer - 1).bit_length())
    halves = width // size if span // outer >= 8 else 1
    chunks = node_local * halves
    wide = width // halves
    f32, bf16 = jnp.float32, jnp.bfloat16
    dma = pltpu.SemaphoreType.DMA
    updated, factor = pl.pallas_call(
        functools.partial(kernel, subs, nodes, inner, halves, sliced),
        out_shape=[
            jax.ShapeDtypeStruct((count, size, col_count), f32),
            jax.ShapeDtypeStruct((1, col_count), f32),
        ],
        in_specs=[pl.BlockSpec(memory_space=SMEM)] * 2
        + [pl.BlockSpec(memory_space=VMEM)] * 2
        + [pl.BlockSpec(memory_space=pl.ANY)] * 4,
        out_specs=[pl.BlockSpec(memory_space=VMEM)] * 2,
        scratch_shapes=[
            VMEM((count, size, col_count), f32),
            VMEM((size, size), f32),
            VMEM(matrix_blocks.shape, f32),
            VMEM(inverses.shape, f32),
            VMEM(panels.shape[1:], f32),
            VMEM((count + 2 * HALO_BLOCKS, size, col_count), f32),
            VMEM((inner, sep_blocks, 8, wide), f32),
            VMEM((nodes, count, size, col_count), f32),
            VMEM(panels.shape[1:], bf16),
            VMEM(panels.shape[1:], bf16),
            VMEM(panels.shape[:0:-1], bf16),
            VMEM(panels.shape[:0:-1], bf16),
            VMEM((node_local, count, size, 2 * size), bf16),
            VMEM((node_local, count, size, 2 * size), bf16),
            VMEM((chunks, count, size, 2 * wide), bf16),
            VMEM((chunks, count, size, 2 * wide), bf16),
            VMEM((chunks, 2, sep_blocks, size, wide), f32),
            VMEM((chunks, inner, 2, sep_blocks, span, wide), f32),
            VMEM((chunks, 2, groups, span, wide), f32),
            VMEM((chunks, rounds, 2, groups, span // 2, wide), f32),
            VMEM((chunks, 2, groups, span, wide), f32),
            VMEM((chunks, inner, 2, sep_blocks, span, wide), f32),
            VMEM((chunks, 2, sep_blocks, size, wide), f32),
            VMEM((count, size, width), f32),
            VMEM((nodes, count, size, col_count), f32),
            VMEM((nodes - 1, count, size, col_count), f32),
            VMEM((subs, 8, col_count), f32),
            dma((5,)),
            dma((2,)),
            dma((2,)),
            dma((inner - 1,)),
            dma((inner - 1,)),
            dma((nodes - 1, count)),
            dma((nodes - 1, count)),
            dma((chunks, 2, inner - 1)),
            dma((chunks, 2, inner - 1)),
            dma((chunks, 2, rounds)),
            dma((chunks, 2, rounds)),
            dma((chunks, 3)),
            dma((nodes - 1, count)),
            dma((nodes - 1, count)),
            dma((subs - 1,)),
            dma((subs - 1,)),
        ],
        compiler_params=pltpu.CompilerParams(
            collective_id=0, has_side_effects=True, vmem_limit_bytes=60 * 1024 * 1024
        ),
        name="update",
    )(
        block_lists, separator_map, ritz_values[None], separator_shift.reshape(groups, size),
        vectors, matrix_blocks, inverses, panels[0],
    )
    return (updated * factor[None]).reshape(row_count, col_count)


def solution(mesh):
    return jax.shard_map(
        shards,
        mesh=mesh,
        in_specs=(
            P("sub", None),
            P(),
            P("sub", None, None, None),
            P("sub", None),
            P("node", None, "sub", None, None),
            P("sub", None, None),
            P("sub", None),
            P(),
        ),
        out_specs=P("sub", "node"),
        check_vma=False,
    )
```

```python
import functools
import math

import jax
import jax.numpy as jnp
from jax import lax
from jax.experimental import pallas as pl
from jax.experimental.pallas import tpu as pltpu
from jax.sharding import PartitionSpec as P

HALO_BLOCKS = 4
SEP_GROUPS = 8
VMEM = pltpu.VMEM
SMEM = pltpu.SMEM


def split(x):
    hi = x.astype(jnp.bfloat16)
    lo = (x - hi.astype(jnp.float32)).astype(jnp.bfloat16)
    return hi, lo


def dot_halves(a, b):
    (a_hi, a_lo), (b_hi, b_lo) = a, b
    dot = functools.partial(jnp.dot, preferred_element_type=jnp.float32)
    return dot(a_hi, b_hi) + (dot(a_hi, b_lo) + dot(a_lo, b_hi))


def dot3(a, b):
    return dot_halves(split(a), split(b))


def meet(targets):
    barrier = pltpu.get_barrier_semaphore()
    for target in targets:
        pl.semaphore_signal(
            barrier, inc=1, device_id=target, device_id_type=pl.DeviceIdType.MESH
        )
    pl.semaphore_wait(barrier, len(targets))


def remote(src, dst, send, recv, target):
    return pltpu.make_async_remote_copy(
        src_ref=src,
        dst_ref=dst,
        send_sem=send,
        recv_sem=recv,
        device_id=target,
        device_id_type=pl.DeviceIdType.MESH,
    )


def inner_size(subs):
    return max(k for k in range(1, subs + 1) if subs % k == 0 and k * k <= subs)


def kernel(
    subs, nodes, inner, halves, sliced,
    index_ref, map_ref, ritz_ref, shift_ref, vectors_hbm, blocks_hbm, inverses_hbm, panel_hbm,
    out_ref, factor_ref,
    own_ref, shift_columns, blocks, inverses, panel, padded, maps, residual,
    panel_hi, panel_lo, turned_hi, turned_lo, fold_hi, fold_lo, guess_hi, guess_lo,
    part, near, dense, far, coarse, picked, back, weighted, shares, landed, sums,
    load_sem, halo_send, halo_recv, map_send, map_recv, node_send, node_recv,
    sep_send, sep_recv, far_send, far_recv, own_sem,
    share_send, share_recv, sum_send, sum_recv,
):
    sub, node = lax.axis_index("sub"), lax.axis_index("node")
    count, size, _ = own_ref.shape
    node_local = inverses.shape[0]
    total_nodes = node_local * nodes
    outer = subs // inner
    sep_blocks = map_ref.shape[1]
    groups = shift_ref.shape[0]
    rounds = far.shape[1]
    span = size // inner
    wide = part.shape[-1]
    width = wide * halves
    place, plane = lax.rem(sub, inner), sub // inner
    base = plane * inner
    near_places = [lax.rem(place + k, inner) for k in range(1, inner)]
    bits = [lax.rem(plane // 2**i, 2) for i in range(rounds)]
    partners = [
        {"sub": (plane + 2**i - 2 * 2**i * bits[i]) * inner + place} for i in range(rounds)
    ]
    other_nodes = [lax.rem(node + k, nodes) for k in range(1, nodes)]
    other_subs = [lax.rem(sub + k, subs) for k in range(1, subs)]
    after, before = lax.rem(sub + 1, subs), lax.rem(sub + subs - 1, subs)

    loads = [
        pltpu.make_async_copy(panel_hbm, panel, load_sem.at[0]),
        pltpu.make_async_copy(inverses_hbm, inverses, load_sem.at[1]),
        pltpu.make_async_copy(blocks_hbm, blocks, load_sem.at[2]),
    ]
    if sliced:
        fetch = vectors_hbm
    else:
        part_cols = vectors_hbm.shape[2] // nodes
        first = pl.multiple_of(node * part_cols, part_cols)
        fetch = vectors_hbm.at[:, :, pl.ds(first, part_cols)]
    fetch = pltpu.make_async_copy(fetch, own_ref, load_sem.at[3])
    fetch.start()
    for load in loads:
        load.start()
    for p in range(sep_blocks):
        value = map_ref[0, p].astype(jnp.float32)
        maps[place, p] = jnp.full(maps.shape[2:], value, jnp.float32)
    ritz_parts = [
        ritz_ref[:, j * own_ref.shape[2] : (j + 1) * own_ref.shape[2]] for j in range(nodes)
    ]
    ritz = ritz_parts[0]
    for j in range(1, nodes):
        ritz = jnp.where(node == j, ritz_parts[j], ritz)
    meet([{"sub": o} for o in other_subs] + [{"node": o} for o in other_nodes])
    fetch.wait()
    halo = [
        remote(
            own_ref.at[pl.ds(count - HALO_BLOCKS, HALO_BLOCKS)],
            padded.at[pl.ds(0, HALO_BLOCKS)],
            halo_send.at[0], halo_recv.at[0], {"sub": after},
        ),
        remote(
            own_ref.at[pl.ds(0, HALO_BLOCKS)],
            padded.at[pl.ds(HALO_BLOCKS + count, HALO_BLOCKS)],
            halo_send.at[1], halo_recv.at[1], {"sub": before},
        ),
    ]
    tell = [
        remote(maps.at[place], maps.at[place], map_send.at[k], map_recv.at[k], {"sub": base + t})
        for k, t in enumerate(near_places)
    ]
    for copy in halo + tell:
        copy.start()
    shift_columns[...] = jnp.concatenate(
        [shift_ref[...], jnp.zeros((size - groups, size), jnp.float32)], axis=0
    ).T

    def constant(values):
        chosen = jnp.float32(values[0])
        for k in range(1, nodes):
            chosen = jnp.where(node == k, jnp.float32(values[k]), chosen)
        return chosen

    angles = [
        [math.pi * (k * node_local + n + 0.5) / total_nodes for k in range(nodes)]
        for n in range(node_local)
    ]
    real_shift = [constant([math.cos(a) for a in row]) for row in angles]
    imag_shift = [constant([math.sin(a) for a in row]) for row in angles]
    real_weight = [constant([2.0 * math.cos(a) / total_nodes for a in row]) for row in angles]
    imag_weight = [constant([2.0 * math.sin(a) / total_nodes for a in row]) for row in angles]

    loads[0].wait()
    for p in range(sep_blocks):
        block = panel[p * size : (p + 1) * size]
        hi, lo = split(block)
        panel_hi[p * size : (p + 1) * size] = hi
        panel_lo[p * size : (p + 1) * size] = lo
    loads[1].wait()
    for n in range(node_local):

        def fold(b, carry):
            real, imag = inverses[n, 0, b], inverses[n, 1, b]
            hi, lo = split(real_weight[n] * real - imag_weight[n] * imag)
            fold_hi[n, b, :, :size], fold_lo[n, b, :, :size] = hi, lo
            hi, lo = split(real_weight[n] * imag + imag_weight[n] * real)
            fold_hi[n, b, :, size:], fold_lo[n, b, :, size:] = hi, lo
            return carry

        lax.fori_loop(0, count, fold, 0)
    loads[2].wait()

    def diagonal(b, carry):
        out_ref[b] = dot3(blocks[b, 0], own_ref[b]) - own_ref[b] * ritz
        return carry

    lax.fori_loop(0, count, diagonal, 0)
    place_own = pltpu.make_async_copy(
        own_ref, padded.at[pl.ds(HALO_BLOCKS, count)], load_sem.at[4]
    )
    place_own.start()
    place_own.wait()
    for copy in halo:
        copy.wait()

    def node_copies(b):
        return [
            remote(
                residual.at[node, b], residual.at[node, b],
                node_send.at[k, b], node_recv.at[k, b], {"node": o},
            )
            for k, o in enumerate(other_nodes)
        ]

    def residual_step(b, carry):
        total = out_ref[b]
        for q in range(1, blocks.shape[1]):
            spot = index_ref[b, q] - sub * count + HALO_BLOCKS
            spot = jnp.clip(spot, 0, padded.shape[0] - 1)
            total = total + dot3(blocks[b, q], padded[spot])
        residual[node, b] = total
        for copy in node_copies(b):
            copy.start()
        return carry

    lax.fori_loop(0, count, residual_step, 0)

    def whole_residual(b):
        return jnp.concatenate([residual[j, b] for j in range(nodes)], axis=1)

    def guess(n):
        def step(b, carry):
            if n == 0:
                for copy in node_copies(b):
                    copy.wait()
            right = split(whole_residual(b))
            for c in range(2):
                hi, lo = split(dot_halves(split(inverses[n, c, b]), right))
                for h in range(halves):
                    k = n * halves + h
                    chosen = slice(h * wide, (h + 1) * wide)
                    spot = slice(c * wide, (c + 1) * wide)
                    guess_hi[k, b, :, spot] = hi[:, chosen]
                    guess_lo[k, b, :, spot] = lo[:, chosen]
            return carry

        lax.fori_loop(0, count, step, 0)

    for copy in tell:
        copy.wait()

    def strip(ref, t):
        return ref.at[:, :, pl.ds(pl.multiple_of(t * span, span), span)]

    def region(level, other=False):
        row, col, row_size, col_size = 0, 0, span, wide
        for i in range(level):
            bit = 1 - bits[i] if other and i == level - 1 else bits[i]
            if row_size >= 16:
                row_size //= 2
                row = row + bit * row_size
            else:
                col_size //= 2
                col = col + bit * col_size
        if not isinstance(row, int):
            row = pl.multiple_of(row, 8)
        if not isinstance(col, int):
            col = pl.multiple_of(col, 128)
        return pl.ds(row, row_size), pl.ds(col, col_size)

    def corner(level):
        row, col = region(level)
        return pl.ds(0, row.size), pl.ds(0, col.size)

    def own_copy(k, src, dst, which):
        return pltpu.make_async_copy(src, dst, own_sem.at[k, which])

    def there_near(k):
        return [
            remote(
                strip(part.at[k], t), near.at[k, place],
                sep_send.at[k, 0, i], sep_recv.at[k, 0, i], {"sub": base + t},
            )
            for i, t in enumerate(near_places)
        ]

    def there_far(k, i):
        return [
            remote(
                dense.at[(k, slice(None), slice(None)) + region(i + 1, True)],
                far.at[(k, i, slice(None), slice(None)) + corner(i + 1)],
                far_send.at[k, 0, i], far_recv.at[k, 0, i], partners[i],
            )
        ]

    def home_far(k, i):
        mine = (k, slice(None), slice(None)) + region(i + 1)
        return [
            remote(
                coarse.at[mine], coarse.at[mine],
                far_send.at[k, 1, i], far_recv.at[k, 1, i], partners[i],
            )
        ]

    def home_near(k):
        return [
            remote(
                picked.at[k, t], strip(back.at[k], place),
                sep_send.at[k, 1, i], sep_recv.at[k, 1, i], {"sub": base + t},
            )
            for i, t in enumerate(near_places)
        ]

    def begin(copies):
        for copy in copies:
            copy.start()

    def finish(copies):
        for copy in copies:
            copy.wait()

    def stage_a(k):
        rights = (
            guess_hi[k].reshape(count * size, 2 * wide),
            guess_lo[k].reshape(count * size, 2 * wide),
        )
        value = dot_halves((panel_hi[...], panel_lo[...]), rights)
        value = value.reshape(sep_blocks, size, 2 * wide)
        part[k, 0] = value[:, :, :wide]
        part[k, 1] = value[:, :, wide:]
        begin(there_near(k))
        own_copy(k, strip(part.at[k], place), near.at[k, place], 0).start()

    def stage_b(k):
        finish(there_near(k))
        own_copy(k, strip(part.at[k], place), near.at[k, place], 0).wait()

        def group(g, carry):
            number = g.astype(jnp.float32)

            def add(t, totals):
                for p in range(sep_blocks):
                    hit = jnp.broadcast_to(maps[t, p, 0:1], (span, wide)) == number
                    totals = tuple(
                        total + jnp.where(hit, near[k, t, c, p], 0.0)
                        for c, total in enumerate(totals)
                    )
                return totals

            zero = jnp.zeros((span, wide), jnp.float32)
            totals = (zero, zero)
            for t in range(inner):
                totals = add(t, totals)
            dense[k, 0, g], dense[k, 1, g] = totals
            return carry

        lax.fori_loop(0, groups, group, 0)
        begin(there_far(k, 0))

    def stage_c(k, i):
        finish(there_far(k, i))
        mine = (k, slice(None), slice(None)) + region(i + 1)
        value = dense[mine] + far[(k, i, slice(None), slice(None)) + corner(i + 1)]
        if i < rounds - 1:
            dense[mine] = value
            begin(there_far(k, i + 1))
            return
        n = k // halves
        row, col = region(rounds)
        first = pl.multiple_of(place * span + row.start, 8)
        columns = shift_columns[pl.ds(first, row.size)]
        for g in range(groups):
            gap = real_shift[n] - columns[:, g : g + 1]
            modulus = gap * gap + imag_shift[n] * imag_shift[n]
            shape = (row.size, col.size)
            by_real = jnp.broadcast_to(gap / modulus, shape)
            by_imag = jnp.broadcast_to(imag_shift[n] / modulus, shape)
            real, imag = value[0, g], value[1, g]
            coarse[k, 0, g, row, col] = real * by_real + imag * by_imag
            coarse[k, 1, g, row, col] = imag * by_real - real * by_imag
        begin(home_far(k, rounds - 1))

    def stage_h(k, i):
        finish(home_far(k, i))
        begin(home_far(k, i - 1))

    def stage_d(k):
        finish(home_far(k, 0))

        def pick(t, carry):
            for p in range(sep_blocks):
                here = jnp.broadcast_to(maps[t, p, 0:1], (span, wide))
                for c in range(2):
                    value = coarse[k, c, 0]
                    for g in range(1, groups):
                        value = jnp.where(here == float(g), coarse[k, c, g], value)
                    picked[k, t, c, p] = value
            return carry

        lax.fori_loop(0, inner, pick, 0)
        begin(home_near(k))
        own_copy(k, picked.at[k, place], strip(back.at[k], place), 2).start()

    def stage_e(k):
        finish(home_near(k))
        own_copy(k, picked.at[k, place], strip(back.at[k], place), 2).wait()
        n, h = divmod(k, halves)
        right = jnp.concatenate(
            [back[k, c].reshape(sep_blocks * size, wide) for c in range(2)], axis=1
        )
        value = dot_halves((turned_hi[...], turned_lo[...]), split(right))
        value = value.reshape(count, size, 2 * wide)
        for b in range(count):
            chosen = slice(h * wide, (h + 1) * wide)
            lower = jnp.concatenate(
                [whole_residual(b)[:, chosen] - value[b, :, :wide], value[b, :, wide:]], axis=0
            )
            new = dot_halves((fold_hi[n, b], fold_lo[n, b]), split(lower))
            if n > 0:
                new = new + weighted[b, :, chosen]
            weighted[b, :, chosen] = new

    def turn(p):
        hi, lo = split(panel[p * size : (p + 1) * size].T)
        turned_hi[:, p * size : (p + 1) * size] = hi
        turned_lo[:, p * size : (p + 1) * size] = lo

    chunks = node_local * halves
    stages = [stage_b]
    stages += [functools.partial(stage_c, i=i) for i in range(rounds)]
    stages += [functools.partial(stage_h, i=i) for i in range(rounds - 1, 0, -1)]
    stages += [stage_d, stage_e]
    for n in range(node_local):
        guess(n)
        for h in range(halves):
            stage_a(n * halves + h)
    for step in range(chunks + len(stages) - 1):
        for s, stage in enumerate(stages):
            if 0 <= step - s < chunks:
                stage(step - s)
        for p in range(sep_blocks):
            if p % (len(stages) - 2) == step:
                turn(p)

    part_cols = width // nodes
    for j in range(nodes):
        shares[j] = weighted[:, :, j * part_cols : (j + 1) * part_cols]

    def share_copies(b):
        return [
            remote(
                shares.at[o, b], landed.at[k, b],
                share_send.at[k, b], share_recv.at[k, b], {"node": o},
            )
            for k, o in enumerate(other_nodes)
        ]

    def share_begin(b, carry):
        begin(share_copies(b))
        return carry

    lax.fori_loop(0, count, share_begin, 0)

    def update_step(b, squares):
        finish(share_copies(b))
        total = own_ref[b] - shares[node, b]
        for k in range(nodes - 1):
            total = total - landed[k, b]
        out_ref[b] = total
        return squares + jnp.sum(total * total, axis=0, keepdims=True)

    squares = lax.fori_loop(0, count, update_step, jnp.zeros((1, part_cols), jnp.float32))
    sums[sub] = jnp.broadcast_to(squares, (8, part_cols))
    spread = [
        remote(sums.at[sub], sums.at[sub], sum_send.at[k], sum_recv.at[k], {"sub": o})
        for k, o in enumerate(other_subs)
    ]
    begin(spread)
    finish(spread)
    total = sums[0]
    for t in range(1, subs):
        total = total + sums[t]
    rows = count * size * subs
    factor_ref[...] = lax.rsqrt(total[0:1] / rows + 1e-06)


def shards(
    search_vectors,
    ritz_values,
    matrix_blocks,
    block_lists,
    inverses,
    panels,
    separator_map,
    separator_shift,
):
    row_count, width = search_vectors.shape
    count, degree, size, _ = matrix_blocks.shape
    nodes, subs = lax.axis_size("node"), lax.axis_size("sub")
    node_local = inverses.shape[0]
    col_count = width // nodes
    vectors = search_vectors
    sliced = col_count % 128 != 0
    if sliced:
        start = lax.axis_index("node") * col_count
        vectors = lax.dynamic_slice_in_dim(vectors, start, col_count, 1)
    vectors = vectors.reshape(count, size, -1)

    inner = inner_size(subs)
    outer = subs // inner
    sep_blocks = separator_map.shape[1]
    groups = separator_shift.shape[0] // size
    span = size // inner
    rounds = max(1, (outer - 1).bit_length())
    halves = width // size if span // outer >= 8 else 1
    chunks = node_local * halves
    wide = width // halves
    f32, bf16 = jnp.float32, jnp.bfloat16
    dma = pltpu.SemaphoreType.DMA
    updated, factor = pl.pallas_call(
        functools.partial(kernel, subs, nodes, inner, halves, sliced),
        out_shape=[
            jax.ShapeDtypeStruct((count, size, col_count), f32),
            jax.ShapeDtypeStruct((1, col_count), f32),
        ],
        in_specs=[pl.BlockSpec(memory_space=SMEM)] * 2
        + [pl.BlockSpec(memory_space=VMEM)] * 2
        + [pl.BlockSpec(memory_space=pl.ANY)] * 4,
        out_specs=[pl.BlockSpec(memory_space=VMEM)] * 2,
        scratch_shapes=[
            VMEM((count, size, col_count), f32),
            VMEM((size, size), f32),
            VMEM(matrix_blocks.shape, f32),
            VMEM(inverses.shape, f32),
            VMEM(panels.shape[1:], f32),
            VMEM((count + 2 * HALO_BLOCKS, size, col_count), f32),
            VMEM((inner, sep_blocks, 8, wide), f32),
            VMEM((nodes, count, size, col_count), f32),
            VMEM(panels.shape[1:], bf16),
            VMEM(panels.shape[1:], bf16),
            VMEM(panels.shape[:0:-1], bf16),
            VMEM(panels.shape[:0:-1], bf16),
            VMEM((node_local, count, size, 2 * size), bf16),
            VMEM((node_local, count, size, 2 * size), bf16),
            VMEM((chunks, count, size, 2 * wide), bf16),
            VMEM((chunks, count, size, 2 * wide), bf16),
            VMEM((chunks, 2, sep_blocks, size, wide), f32),
            VMEM((chunks, inner, 2, sep_blocks, span, wide), f32),
            VMEM((chunks, 2, groups, span, wide), f32),
            VMEM((chunks, rounds, 2, groups, span // 2, wide), f32),
            VMEM((chunks, 2, groups, span, wide), f32),
            VMEM((chunks, inner, 2, sep_blocks, span, wide), f32),
            VMEM((chunks, 2, sep_blocks, size, wide), f32),
            VMEM((count, size, width), f32),
            VMEM((nodes, count, size, col_count), f32),
            VMEM((nodes - 1, count, size, col_count), f32),
            VMEM((subs, 8, col_count), f32),
            dma((5,)),
            dma((2,)),
            dma((2,)),
            dma((inner - 1,)),
            dma((inner - 1,)),
            dma((nodes - 1, count)),
            dma((nodes - 1, count)),
            dma((chunks, 2, inner - 1)),
            dma((chunks, 2, inner - 1)),
            dma((chunks, 2, rounds)),
            dma((chunks, 2, rounds)),
            dma((chunks, 3)),
            dma((nodes - 1, count)),
            dma((nodes - 1, count)),
            dma((subs - 1,)),
            dma((subs - 1,)),
        ],
        compiler_params=pltpu.CompilerParams(
            collective_id=0, has_side_effects=True, vmem_limit_bytes=60 * 1024 * 1024
        ),
        name="update",
    )(
        block_lists, separator_map, ritz_values[None], separator_shift.reshape(groups, size),
        vectors, matrix_blocks, inverses, panels[0],
    )
    return (updated * factor[None]).reshape(row_count, col_count)


def solution(mesh):
    return jax.shard_map(
        shards,
        mesh=mesh,
        in_specs=(
            P("sub", None),
            P(),
            P("sub", None, None, None),
            P("sub", None),
            P("node", None, "sub", None, None),
            P("sub", None, None),
            P("sub", None),
            P(),
        ),
        out_specs=P("sub", "node"),
        check_vma=False,
    )
```
